512 devices in a mesh: block: 32 (over x, z), token: 16 (over y, core).
Axes of the slice: x: 4, y: 8, z: 8, core: 2. Of those that a mesh axis runs over, the one named last changes fastest.
Arguments:
- voxel_feats: bfloat16 [96, 524288], P(None, ('block', 'token')), may hold values from -6 to 6
- occupancy: int32 [524288], P(('block', 'token')), may hold values 0 or 1
- adjacency: int32 [2, 6, 1024], P(None, None, ('block', 'token')), may hold values from -1 to 31, as said below
- serial_pos: int32 [524288], P(('block', 'token')), may hold values from 0 to 16383, as said below
- conv_one: bfloat16 [7, 96, 96], replicated, may hold values from -0.25 to 0.25
- conv_two: bfloat16 [7, 96, 96], replicated, may hold values from -0.25 to 0.25
- gain_one: float32 [96], replicated, may hold values from 0.25 to 1.75
- gain_two: float32 [96], replicated, may hold values from 0.25 to 1.75
- gain_attn: float32 [96], replicated, may hold values from 0.25 to 1.75
- w_qkv: bfloat16 [144, 96], replicated, may hold values from -2 to 2
- w_out: bfloat16 [96, 48], replicated, may hold values from -4 to 4
- gain_mlp: float32 [96], replicated, may hold values from 0.25 to 1.75
- w_up: bfloat16 [384, 96], replicated, may hold values from -0.625 to 0.625
- w_down: bfloat16 [96, 384], replicated, may hold values from -0.3125 to 0.3125
Outputs:
- voxel_out: bfloat16 [96, 524288], P(None, ('block', 'token'))
The draws below stay inside these ranges and needn't reach their ends.
Inputs may be any that keep to these rules, and one draw needn't show every extreme that they name: adjacency[0, f, g] is the segment of the neighbour of block g across face f, or -1 where there is none, and adjacency[1, f, g] is that neighbour's index among its device's 2 blocks (-1 with it). Neighbours lie in the same frame and at most 2 segments away; if block g' is the neighbour of g across face f, then g is the neighbour of g' across face f xor 1. At most 2 faces of one device have their neighbours on one other device. Within each group of rows k * 16384 to (k + 1) * 16384 - 1 (one segment of every frame), serial_pos is a permutation of 0 to 16383. At most 128 rows of one device take positions of any one device's range of 1024 positions, its own included.
All inputs are finite; a program needn't handle non-finite values. No bound on the sum of `occupancy` on one device may be relied on, other than what follows from the above.
Results may differ from the reference program's by a relative error of at most 0.04.
Values may be sent and summed in bfloat16 or wider, within the bound.
A program may use at most 64 MiB of HBM per device.

```python
import math
import jax
import jax.numpy as jnp
from jax import lax

C = 96
HEADS = 6
HD = 8
FFN = 384
EDGE = 8
PATCH = 512
BLK_DEV = 2
TOK_DEV = 1024
SEGS = 32
FRAMES = 16
NBLK = 1024
ROWS = 524288
ROWS_GRP = 16384
ROW_CAP = 128


def axis_links(link_key, stay_count, near_count):
    sub_keys = jax.random.split(link_key, 2)
    total_blocks = SEGS * BLK_DEV
    places = jnp.arange(BLK_DEV, dtype=jnp.int32)
    offsets = (places >= stay_count).astype(jnp.int32) + (places >= stay_count + near_count).astype(jnp.int32)
    shuffles = jax.vmap(lambda sub_key: jax.random.permutation(sub_key, BLK_DEV).astype(jnp.int32))(jax.random.split(sub_keys[0], SEGS))
    steps_out = offsets[shuffles]
    segments = jnp.arange(SEGS, dtype=jnp.int32)[:, None]
    reached = (segments + steps_out).reshape(-1)
    target_seg = reached % SEGS
    source = (segments * BLK_DEV + places[None, :]).reshape(-1)
    ordering = jnp.argsort(target_seg * total_blocks + source)
    rank_of = jnp.zeros((total_blocks,), jnp.int32).at[ordering].set(jnp.arange(total_blocks, dtype=jnp.int32))
    within = rank_of - target_seg * BLK_DEV
    arrivals = jax.vmap(lambda sub_key: jax.random.permutation(sub_key, BLK_DEV).astype(jnp.int32))(jax.random.split(sub_keys[1], SEGS))
    target_slot = arrivals[target_seg, within]
    target = target_seg * BLK_DEV + target_slot
    linked = (reached < SEGS) & (target != source)
    plus_owner = jnp.where(linked, target_seg, -1)
    plus_slot = jnp.where(linked, target_slot, -1)
    unlinked = jnp.full((total_blocks,), -1, jnp.int32)
    minus_owner = unlinked.at[target].set(jnp.where(linked, source // BLK_DEV, -1))
    minus_slot = unlinked.at[target].set(jnp.where(linked, source % BLK_DEV, -1))
    return (jnp.stack([minus_owner, plus_owner]), jnp.stack([minus_slot, plus_slot]))


def frame_links(frame_key):
    sub_keys = jax.random.split(frame_key, 3)
    cut_points = jnp.sort(jax.random.randint(sub_keys[0], (2,), 0, BLK_DEV + 1))
    near_count = jnp.stack([cut_points[0], cut_points[1] - cut_points[0], BLK_DEV - cut_points[1]]).astype(jnp.int32)
    room_left = jnp.minimum(near_count, BLK_DEV - near_count)
    far_count = jax.random.randint(sub_keys[1], (3,), 0, room_left + 1).astype(jnp.int32)
    stay_count = BLK_DEV - near_count - far_count
    axis_keys = jax.random.split(sub_keys[2], 3)
    owner_rows = []
    slot_rows = []
    for axis_index in range(3):
        owner_pair, slot_pair = axis_links(axis_keys[axis_index], stay_count[axis_index], near_count[axis_index])
        owner_rows.append(owner_pair)
        slot_rows.append(slot_pair)
    owners = jnp.concatenate(owner_rows).reshape(6, SEGS, BLK_DEV)
    slots_all = jnp.concatenate(slot_rows).reshape(6, SEGS, BLK_DEV)
    return jnp.stack([owners, slots_all])


def draw_adjacency(key, part):
    frame_keys = jax.random.split(jax.random.fold_in(key, 7), FRAMES)
    links = jax.vmap(frame_links)(frame_keys)
    return jnp.transpose(links, (1, 2, 3, 0, 4)).reshape(2, 6, NBLK).astype(jnp.int32)


def group_order(group_key):
    sub_keys = jax.random.split(group_key, 4)
    halves = jax.random.randint(sub_keys[0], (FRAMES // 2,), 0, ROW_CAP + 1).astype(jnp.int32).at[1].set(ROW_CAP)
    counts = jnp.stack([halves, ROW_CAP - halves], axis=1).reshape(FRAMES)
    labels = jnp.repeat(jnp.arange(FRAMES, dtype=jnp.int32), counts, total_repeat_length=TOK_DEV)
    rotation = jax.random.permutation(sub_keys[1], FRAMES).astype(jnp.int32)
    inverse_rotation = jnp.zeros((FRAMES,), jnp.int32).at[rotation].set(jnp.arange(FRAMES, dtype=jnp.int32))
    shuffles = jax.vmap(lambda sub_key: jax.random.permutation(sub_key, TOK_DEV).astype(jnp.int32))(jax.random.split(sub_keys[2], FRAMES))
    frames_col = jnp.arange(FRAMES, dtype=jnp.int32)[:, None]
    target_dev = inverse_rotation[(rotation[frames_col] + labels[shuffles]) % FRAMES].reshape(-1)
    total_rows = FRAMES * TOK_DEV
    source = jnp.arange(total_rows, dtype=jnp.int32)
    ordering = jnp.argsort(target_dev * total_rows + source)
    rank_of = jnp.zeros((total_rows,), jnp.int32).at[ordering].set(jnp.arange(total_rows, dtype=jnp.int32))
    within = rank_of - target_dev * TOK_DEV
    places = jax.vmap(lambda sub_key: jax.random.permutation(sub_key, TOK_DEV).astype(jnp.int32))(jax.random.split(sub_keys[3], FRAMES))
    return target_dev * TOK_DEV + places[target_dev, within]


def draw_serial_pos(key, part):
    group_keys = jax.random.split(jax.random.fold_in(key, 5), SEGS)
    orders = jax.vmap(group_order)(group_keys)
    return orders.reshape(ROWS).astype(jnp.int32)


def draw_w_qkv(key, part):
    first_key = jax.random.fold_in(jax.random.fold_in(key, 3), 0)
    width_heads = HEADS * HD
    matrix = jax.random.normal(first_key, (3 * width_heads, C), jnp.float32) / math.sqrt(C)
    matrix = jnp.clip(matrix, -2.0, 2.0)
    return matrix.astype(jnp.bfloat16)


def set_ends(entries, stream_key, least, high):
    longest = entries.shape.index(max(entries.shape))
    spots = []
    for shift in (0, 1):
        where = [jax.random.randint(jax.random.fold_in(stream_key, axis), (), 0, length) for axis, length in enumerate(entries.shape)]
        where[longest] = (where[longest] + shift) % entries.shape[longest]
        spots.append(tuple(where))
    return entries.at[spots[0]].set(least).at[spots[1]].set(high)


def level_of(stream_key, dims, pieces, low, high):
    def one(dim, parts):
        steps = jax.random.uniform(jax.random.fold_in(jax.random.fold_in(stream_key, 6), dim), (parts,), jnp.float32, low / len(pieces), high / len(pieces))
        return jnp.repeat(jnp.exp(steps), dims[dim] // parts).reshape((-1,) + (1,) * (len(dims) - dim - 1))

    factor_of = one(*pieces[0])
    for cut in pieces[1:]:
        factor_of = factor_of * one(*cut)
    return factor_of


def centred(own_key, dims, scale, reach, pieces=(), held_as=jnp.bfloat16):
    values = scale * jax.random.normal(own_key, dims, jnp.float32)
    if pieces:
        values = values * level_of(own_key, dims, pieces, -0.22, 0.18)
    return jnp.clip(values, -reach, reach).astype(held_as)


def setup_inputs(seed: int = 0) -> dict:
    splits = jax.random.split(jax.random.key(seed), 15)
    voxel_feats = centred(splits[0], (C, ROWS), 1.0, 6.0, ((1, 512),))
    occupancy = set_ends((jax.random.randint(splits[1], (ROWS,), 0, 5) < 3).astype(jnp.int32), jax.random.fold_in(splits[1], 1), 0, 1)
    adjacency = draw_adjacency(jax.random.fold_in(splits[14], 71), 0)
    serial_pos = draw_serial_pos(jax.random.fold_in(splits[14], 71), 0)
    conv_one = centred(splits[4], (7, C, C), (7 * C) ** -0.5, 0.25)
    conv_two = centred(splits[5], (7, C, C), (7 * C) ** -0.5, 0.25)
    gain_one = jnp.clip(1.0 + 0.15 * jax.random.normal(splits[6], (C,), jnp.float32), 0.25, 1.75)
    gain_two = jnp.clip(1.0 + 0.15 * jax.random.normal(splits[7], (C,), jnp.float32), 0.25, 1.75)
    gain_attn = jnp.clip(1.0 + 0.15 * jax.random.normal(splits[8], (C,), jnp.float32), 0.25, 1.75)
    w_qkv = draw_w_qkv(jax.random.fold_in(splits[14], 71), 0)
    w_out = centred(splits[10], (C, HEADS * HD), 0.3, 4.0)
    gain_mlp = jnp.clip(1.0 + 0.15 * jax.random.normal(splits[11], (C,), jnp.float32), 0.25, 1.75)
    w_up = centred(splits[12], (FFN, C), C ** -0.5, 0.625)
    w_down = centred(splits[13], (C, FFN), FFN ** -0.5, 0.3125)
    return dict(voxel_feats=voxel_feats, occupancy=occupancy, adjacency=adjacency, serial_pos=serial_pos, conv_one=conv_one, conv_two=conv_two, gain_one=gain_one, gain_two=gain_two, gain_attn=gain_attn, w_qkv=w_qkv, w_out=w_out, gain_mlp=gain_mlp, w_up=w_up, w_down=w_down)


EPS = 1e-05
FLIP = (1, 0, 3, 2, 5, 4)

def layer_norm(values, gain):
    center = values - lax.optimization_barrier(jnp.mean(values, axis=0, keepdims=True))
    spread = lax.optimization_barrier(jnp.mean(center * center, axis=0, keepdims=True))
    return center * lax.rsqrt(spread + EPS) * gain[:, None]

def face_layers(voxels):
    blocks_here = voxels.shape[1]
    face_list = [voxels[:, :, 0], voxels[:, :, -1], voxels[:, :, :, 0], voxels[:, :, :, -1], voxels[:, :, :, :, 0], voxels[:, :, :, :, -1]]
    return jnp.stack([jnp.transpose(face_layer, (1, 0, 2, 3)).reshape(blocks_here, -1) for face_layer in face_list])

def shifted_taps(voxels, halo_cube):
    return [voxels, jnp.concatenate([halo_cube[0][:, :, None], voxels[:, :, :-1]], axis=2), jnp.concatenate([voxels[:, :, 1:], halo_cube[1][:, :, None]], axis=2), jnp.concatenate([halo_cube[2][:, :, :, None], voxels[:, :, :, :-1]], axis=3), jnp.concatenate([voxels[:, :, :, 1:], halo_cube[3][:, :, :, None]], axis=3), jnp.concatenate([halo_cube[4][..., None], voxels[..., :-1]], axis=4), jnp.concatenate([voxels[..., 1:], halo_cube[5][..., None]], axis=4)]

def reference_halo(signal, adjacency):
    channels = signal.shape[0]
    voxels = signal.reshape(channels, NBLK, EDGE, EDGE, EDGE)
    faces = face_layers(voxels).reshape(6 * NBLK, -1)
    owners = adjacency[0]
    indices = adjacency[1]
    block_ids = jnp.arange(NBLK, dtype=jnp.int32)
    frame_ids = block_ids // BLK_DEV % FRAMES
    neighbour = (owners * FRAMES + frame_ids[None, :]) * BLK_DEV + indices
    flipped = jnp.array(FLIP, dtype=jnp.int32)
    position = flipped[:, None] * NBLK + neighbour
    present = owners >= 0
    picked = jnp.take(faces, jnp.where(present, position, 0).reshape(-1), axis=0)
    picked = jnp.where(present.reshape(-1, 1), picked, jnp.zeros_like(picked))
    return picked.reshape(6, NBLK, -1)

def cross_conv(signal, weight, halo_flat):
    channels = signal.shape[0]
    blocks_all = halo_flat.shape[1]
    voxels = signal.reshape(channels, blocks_all, EDGE, EDGE, EDGE)
    halo_cube = jnp.transpose(halo_flat.reshape(6, blocks_all, channels, EDGE, EDGE), (0, 2, 1, 3, 4))
    taps_list = shifted_taps(voxels, halo_cube)
    accumulated = jnp.zeros(signal.shape, jnp.float32)
    for tap_index in range(7):
        accumulated = accumulated + jnp.dot(weight[tap_index], taps_list[tap_index].reshape(channels, -1), preferred_element_type=jnp.float32)
    return accumulated

def patch_attention(patch_rows, live_keys, w_qkv):
    width_heads = HEADS * HD
    projected = jnp.dot(w_qkv, patch_rows, preferred_element_type=jnp.float32)
    queries = projected[:width_heads].reshape(HEADS, HD, -1)
    keys_all = projected[width_heads:2 * width_heads].reshape(HEADS, HD, -1)
    values_all = projected[2 * width_heads:].astype(jnp.bfloat16).reshape(HEADS, HD, -1)
    scores = jnp.einsum('hdq,hdk->hqk', queries, keys_all, precision=lax.Precision.HIGHEST) * HD ** (-0.5)
    allowed = (live_keys[None, :] > 0) | jnp.eye(PATCH, dtype=bool)
    scores = jnp.where(allowed[None], scores, -jnp.inf)
    largest = lax.optimization_barrier(jnp.max(scores, axis=-1, keepdims=True))
    weights = jnp.exp(scores - largest)
    probability = (weights / lax.optimization_barrier(jnp.sum(weights, axis=-1, keepdims=True))).astype(jnp.bfloat16)
    result = jnp.einsum('hqk,hdk->hdq', probability.astype(jnp.float32), values_all.astype(jnp.float32))
    return result.astype(jnp.bfloat16).reshape(width_heads, -1)

def mlp_tail(combined_part, live_part, gain_mlp, w_up, w_down):
    tail_in = layer_norm(combined_part, gain_mlp).astype(jnp.bfloat16)
    hidden = jax.nn.gelu(jnp.dot(w_up, tail_in, preferred_element_type=jnp.float32)).astype(jnp.bfloat16)
    summed = combined_part + jnp.dot(w_down, hidden, preferred_element_type=jnp.float32)
    return jnp.where(live_part[None, :] > 0, summed, 0.0).astype(jnp.bfloat16)

def reference(voxel_feats, occupancy, adjacency, serial_pos, conv_one, conv_two, gain_one, gain_two, gain_attn, w_qkv, w_out, gain_mlp, w_up, w_down):
    channels = voxel_feats.shape[0]
    present = occupancy[None, :] > 0
    signal = jnp.where(present, voxel_feats, jnp.zeros_like(voxel_feats))
    first_conv = cross_conv(signal, conv_one, reference_halo(signal, adjacency))
    middle = jnp.where(present, jax.nn.relu(layer_norm(first_conv, gain_one)), 0.0).astype(jnp.bfloat16)
    second_conv = cross_conv(middle, conv_two, reference_halo(middle, adjacency))
    block_out = jnp.where(present, jax.nn.relu(signal.astype(jnp.float32) + layer_norm(second_conv, gain_two)), 0.0).astype(jnp.bfloat16)
    row_ids = jnp.arange(ROWS, dtype=jnp.int32)
    place = (row_ids // ROWS_GRP * ROWS_GRP + serial_pos).astype(jnp.int32)
    serial = jnp.zeros_like(block_out).at[:, place].set(block_out)
    serial_live = jnp.zeros((ROWS,), jnp.int32).at[place].set(occupancy)
    normed = layer_norm(serial.astype(jnp.float32), gain_attn).astype(jnp.bfloat16)
    patch_count = ROWS // PATCH
    patches = jnp.transpose(normed.reshape(channels, patch_count, PATCH), (1, 0, 2))
    live_patches = serial_live.reshape(patch_count, PATCH)
    heads_out = lax.map(lambda pair_item: patch_attention(pair_item[0], pair_item[1], w_qkv), (patches, live_patches))
    width_heads = HEADS * HD
    heads_out = jnp.transpose(heads_out, (1, 0, 2)).reshape(width_heads, ROWS)
    attended = jnp.dot(w_out, heads_out, preferred_element_type=jnp.float32).astype(jnp.bfloat16)
    returned = attended[:, place]
    combined = block_out.astype(jnp.float32) + returned.astype(jnp.float32)
    span_count = ROWS // TOK_DEV
    stacked = jnp.transpose(combined.reshape(channels, span_count, TOK_DEV), (1, 0, 2))
    live_spans = occupancy.reshape(span_count, TOK_DEV)
    tail_out = lax.map(lambda pair_item: mlp_tail(pair_item[0], pair_item[1], gain_mlp, w_up, w_down), (stacked, live_spans))
    return jnp.transpose(tail_out, (1, 0, 2)).reshape(channels, ROWS)
```

```python
import functools
import math

import jax
import jax.numpy as jnp
from jax import lax
from jax.experimental import pallas as pl
from jax.experimental.pallas import tpu as pltpu
from jax.sharding import PartitionSpec as P

MESH = pl.DeviceIdType.MESH
F32 = jnp.float32
BF16 = jnp.bfloat16
I32 = jnp.int32

HEADS = 6
HD = 8
PATCH = 512
BLOCK = 512
FACE = 64
EPS = 1e-05
OFFS = (-2, -1, 1, 2)
SHIFTS = (64, -64, 8, -8, 1, -1)
AWAY = -1e30
NT_DIMS = (((1,), (1,)), ((), ()))
QROWS = 256
GROUP = 4


def dot(a, b):
    return jnp.dot(a, b, preferred_element_type=F32)


def dot_nt(a, b):
    return lax.dot_general(a, b, NT_DIMS, preferred_element_type=F32)


def face_index(face, place):
    high, low = place >> 3, place & 7
    if face == 0:
        return place
    if face == 1:
        return place + 448
    if face == 2:
        return high * 64 + low
    if face == 3:
        return high * 64 + low + 56
    if face == 4:
        return place * 8
    return place * 8 + 7


def store_one_hot(ref, row0, rows, lanes, index):
    width = index.shape[1]
    places = lax.broadcasted_iota(I32, (128, width), 0).astype(F32).astype(BF16)
    for part in range(rows // 128):
        here = jnp.where(index >> 7 == part, index & 127, -1).astype(F32).astype(BF16)
        hit = jnp.where(places == here, jnp.ones((), BF16), jnp.zeros((), BF16))
        ref[row0 + part * 128 : row0 + (part + 1) * 128, lanes] = hit


def column_of(row):
    size = row.shape[1]
    same = lax.broadcasted_iota(I32, (size, size), 0) == lax.broadcasted_iota(I32, (size, size), 1)
    return jnp.sum(jnp.where(same, row, 0.0), axis=1, keepdims=True)


def normalise(values, gain):
    center = values - jnp.mean(values, axis=0, keepdims=True)
    spread = jnp.mean(center * center, axis=0, keepdims=True)
    return center * lax.rsqrt(spread + EPS) * gain


def kernel(
    nb,
    nt,
    feats,
    occupancy,
    adjacency,
    serial_pos,
    conv_one,
    conv_two,
    gain_one,
    gain_two,
    gain_attn,
    w_qkv,
    w_out,
    gain_mlp,
    w_up,
    w_down,
    out_ref,
    signal,
    taps,
    conv_cat,
    send_pick,
    remote_pick,
    local_pick,
    spread_pick,
    halo_send,
    halo_recv,
    pack,
    label_send,
    label_recv,
    live_rows,
    place,
    block_out,
    data_send,
    data_recv,
    serial_acc,
    key_rows,
    query_rows,
    value_rows,
    self_rows,
    heads_out,
    back_send,
    back_recv,
    halo_sems,
    label_sems,
    data_sems,
    back_sems,
):
    channels, rows = feats.shape
    cap = pack.shape[0] // nt
    me_b = lax.axis_index("block")
    me_t = lax.axis_index("token")

    barrier = pltpu.get_barrier_semaphore()
    for off in OFFS:
        pl.semaphore_signal(
            barrier, inc=1, device_id={"block": lax.rem(me_b + off + nb, nb)}, device_id_type=MESH
        )
    for k in range(1, nt):
        pl.semaphore_signal(
            barrier, inc=1, device_id={"token": lax.rem(me_t + k, nt)}, device_id_type=MESH
        )

    def halo_copy(step, o):
        return pltpu.make_async_remote_copy(
            src_ref=halo_send.at[step, o],
            dst_ref=halo_recv.at[step, o],
            send_sem=halo_sems.at[0, step, o],
            recv_sem=halo_sems.at[1, step, o],
            device_id={"block": lax.rem(me_b + OFFS[o] + nb, nb)},
            device_id_type=MESH,
        )

    def token_copy(source, target, sems, k, step):
        return pltpu.make_async_remote_copy(
            src_ref=source.at[k],
            dst_ref=target.at[k],
            send_sem=sems.at[0, k],
            recv_sem=sems.at[1, k],
            device_id={"token": lax.rem(me_t + step + nt, nt)},
            device_id_type=MESH,
        )

    label_copy = lambda k: token_copy(label_send, label_recv, label_sems, k, k)
    data_copy = lambda k: token_copy(data_send, data_recv, data_sems, k, k)
    back_copy = lambda k: token_copy(back_send, back_recv, back_sems, k, -k)

    owner = {}
    index = {}
    for f in range(6):
        for b in range(2):
            owner[f, b] = adjacency[0, f, b]
            index[f, b] = adjacency[1, f, b]
    pairs = [(f, b) for f in range(6) for b in range(2)]
    lane = lax.broadcasted_iota(I32, (1, 128), 1)
    half, within = lane >> 6, lane & 63
    voxel_of = [face_index(f, within) for f in range(6)]
    for o, off in enumerate(OFFS):
        target = me_b + off
        count = jnp.int32(0)
        voxel = jnp.full((1, 128), -1, I32)
        for f, b in pairs:
            match = (owner[f, b] >= 0) & (owner[f, b] == target)
            slot = jnp.where(match, count, -1)
            count = count + jnp.where(match, 1, 0)
            voxel = jnp.where(half == slot, voxel_of[f] + b * BLOCK, voxel)
        store_one_hot(send_pick, 0, rows, slice(o * 128, (o + 1) * 128), voxel)

    occupied = occupancy[...] > 0
    field = jnp.where(occupied, feats[...].astype(F32), 0.0)
    signal[...] = field.astype(BF16)

    def send_halo(step):
        payload = dot(signal[...] if step == 0 else taps[0:channels, :], send_pick[...]).astype(BF16)
        for o in range(4):
            halo_send[step, o] = payload[:, o * 128 : (o + 1) * 128]

    send_halo(0)

    position = serial_pos[...]
    relative = ((position >> 10) - me_t + nt) & (nt - 1)
    sub16 = lax.broadcasted_iota(I32, (16, rows), 0)
    member = jnp.where(sub16 == relative, 1.0, 0.0)
    upto = lax.broadcasted_iota(I32, (128, 128), 0) <= lax.broadcasted_iota(I32, (128, 128), 1)
    upto = jnp.where(upto, 1.0, 0.0).astype(BF16)
    chunks = rows // 128
    stacked = jnp.concatenate(
        [member[:, c * 128 : (c + 1) * 128] for c in range(chunks)], axis=0
    ).astype(BF16)
    prefix = dot(stacked, upto)
    carry = jnp.zeros((16, 1), F32)
    ranks = []
    for c in range(chunks):
        piece = prefix[c * 16 : (c + 1) * 16, :]
        ranks.append(piece + carry - 1.0)
        carry = carry + piece[:, 127:128]
    slots = jnp.where(member > 0.5, jnp.concatenate(ranks, axis=1), -1.0).astype(I32)
    for k in range(nt):
        store_one_hot(pack, k * cap, cap, slice(0, rows), slots[k : k + 1, :])
    target_row = position & (rows - 1)
    facts = jnp.where(
        sub16 == 0,
        target_row >> 5,
        jnp.where(
            sub16 == 1,
            target_row & 31,
            jnp.where(sub16 == 2, jnp.where(occupied, 1, 0), jnp.where(sub16 == 3, 1, 0)),
        ),
    )
    facts = dot_nt(facts.astype(F32).astype(BF16), pack[...])
    goes_to = jnp.where(facts[3:4, :] > 0.5, facts[0:1, :] * 32.0 + facts[1:2, :], -1.0)
    sub8 = lax.broadcasted_iota(I32, (8, goes_to.shape[1]), 0)
    labels = jnp.where(sub8 == 0, goes_to, jnp.where(sub8 == 1, facts[2:3, :], 0.0))
    for k in range(nt):
        part = labels[:, k * cap : (k + 1) * cap]
        if k == 0:
            label_recv[0] = part
        else:
            label_send[k] = part

    pl.semaphore_wait(barrier, 4 + nt - 1)

    for o in range(4):
        halo_copy(0, o).start()
    for k in range(1, nt):
        label_copy(k).start()

    for a in range(3):
        for b in range(2):
            remote_src = jnp.full((1, 128), -1, I32)
            local_src = jnp.full((1, 128), -1, I32)
            for side in range(2):
                f = 2 * a + side
                own, idx = owner[f, b], index[f, b]
                key = (f ^ 1) * 2 + idx
                slot = jnp.int32(0)
                for f2, b2 in pairs:
                    if (f2, b2) != (f, b):
                        before = (owner[f2, b2] == own) & ((f2 ^ 1) * 2 + index[f2, b2] < key)
                        slot = slot + jnp.where(before, 1, 0)
                gap = me_b - own
                from_o = jnp.where(gap < 0, gap + 2, gap + 1)
                remote = (own >= 0) & (gap != 0)
                base = jnp.where(remote, from_o * 128 + slot * FACE, -4096)
                remote_src = jnp.where(half == side, within + base, remote_src)
                base = jnp.where((own >= 0) & (gap == 0), idx * BLOCK, -4096)
                local_src = jnp.where(half == side, voxel_of[f ^ 1] + base, local_src)
            lanes = slice((a * 2 + b) * 128, (a * 2 + b + 1) * 128)
            store_one_hot(remote_pick, 0, 512, lanes, remote_src)
            store_one_hot(local_pick, 0, rows, lanes, local_src)
    side_row = lax.broadcasted_iota(I32, (128, BLOCK), 0)
    voxel_lane = lax.broadcasted_iota(I32, (128, BLOCK), 1)
    for a in (1, 2):
        lower = face_index(2 * a, side_row & 63)
        upper = face_index(2 * a + 1, side_row & 63)
        hit = voxel_lane == jnp.where(side_row < 64, lower, upper)
        spread_pick[a - 1] = jnp.where(hit, 1.0, 0.0).astype(BF16)

    spot = lax.broadcasted_iota(I32, (1, rows), 1) & (BLOCK - 1)
    edges = [spot < 64, spot >= 448, (spot >> 3) & 7 == 0, (spot >> 3) & 7 == 7, spot & 7 == 0, spot & 7 == 7]
    on_edge = [jnp.where(e, 1.0, 0.0) for e in edges]

    def convolve(step, source, weight):
        for t in range(7):
            conv_cat[:, t * channels : (t + 1) * channels] = weight[t]
        for f in range(6):
            moved = pltpu.roll(source, SHIFTS[f] % rows, 1) * (1.0 - on_edge[f])
            taps[(f + 1) * channels : (f + 2) * channels, :] = moved.astype(BF16)
        halo = dot(taps[0:channels, :], local_pick[...])
        for o in range(4):
            halo_copy(step, o).wait_recv()
        received = jnp.concatenate([halo_recv[step, o] for o in range(4)], axis=1)
        halo = (halo + dot(received, remote_pick[...])).astype(BF16)
        for a in range(3):
            for b in range(2):
                lanes = slice((a * 2 + b) * 128, (a * 2 + b + 1) * 128)
                piece = halo[:, lanes]
                if a == 0:
                    gap = jnp.zeros((channels, BLOCK - 256), BF16)
                    wide = jnp.concatenate([piece, gap, piece], axis=1)
                else:
                    wide = dot(piece, spread_pick[a - 1]).astype(BF16)
                cols = slice(b * BLOCK, (b + 1) * BLOCK)
                for side in range(2):
                    f = 2 * a + side
                    tap_rows = slice((f + 1) * channels, (f + 2) * channels)
                    taps[tap_rows, cols] = taps[tap_rows, cols] + wide * on_edge[f][:, cols].astype(BF16)
        return dot(conv_cat[...], taps[...])

    taps[0:channels, :] = signal[...]
    summed = convolve(0, field, conv_one)
    middle = jnp.where(occupied, jnp.maximum(normalise(summed, column_of(gain_one[...])), 0.0), 0.0)
    middle = middle.astype(BF16)
    taps[0:channels, :] = middle
    send_halo(1)
    for o in range(4):
        halo_copy(1, o).start()

    for k in range(1, nt):
        label_copy(k).wait_recv()
    for k in range(nt):
        label = label_recv[k]
        lanes = slice(k * cap, (k + 1) * cap)
        store_one_hot(place, 0, rows, lanes, label[0:1, :].astype(I32))
        live_rows[:, lanes] = jnp.broadcast_to(label[1:2, :], (16, cap)).astype(BF16)
    query_rows[...] = jnp.zeros_like(query_rows)

    summed = convolve(1, middle.astype(F32), conv_two)
    result = jnp.maximum(signal[...].astype(F32) + normalise(summed, column_of(gain_two[...])), 0.0)
    result = jnp.where(occupied, result, 0.0).astype(BF16)
    block_out[...] = result
    normed = normalise(result.astype(F32), column_of(gain_attn[...])).astype(BF16)

    for g in range(nt // GROUP):
        span = slice(g * GROUP * cap, (g + 1) * GROUP * cap)
        packed = dot_nt(normed, pack[span, :]).astype(BF16)
        for j in range(GROUP):
            k = g * GROUP + j
            part = packed[:, j * cap : (j + 1) * cap]
            if k == 0:
                data_recv[0] = part
            else:
                data_send[k] = part
                data_copy(k).start()
    for g in range(nt // GROUP):
        span = slice(g * GROUP * cap, (g + 1) * GROUP * cap)
        for j in range(GROUP):
            if g + j:
                data_copy(g * GROUP + j).wait_recv()
        came = jnp.concatenate([data_recv[g * GROUP + j] for j in range(GROUP)], axis=1)
        came = jnp.concatenate([came, live_rows[:, span]], axis=0)
        part = dot_nt(came, place[:, span])
        serial_acc[...] = part if g == 0 else serial_acc[...] + part

    live = serial_acc[channels : channels + 1, :] > 0.5
    width = HEADS * HD
    projected = dot(w_qkv[...], serial_acc[0:channels, :].astype(BF16))
    scaled = projected[:width, :] * (math.log2(math.e) / math.sqrt(HD))
    query_high = scaled.astype(BF16).astype(F32)
    query_low = scaled - query_high
    keys = projected[width : 2 * width, :]
    key_high = keys.astype(BF16).astype(F32)
    key_low = keys - key_high
    values = projected[2 * width :, :]
    sub8 = lax.broadcasted_iota(I32, (8, rows), 0)
    ones8 = jnp.where(sub8 == 0, 1.0, 0.0)
    bias8 = jnp.where((sub8 == 0) & jnp.logical_not(live), AWAY, 0.0)
    key_parts = []
    patches = rows // PATCH
    for h in range(HEADS):
        own = slice(h * HD, (h + 1) * HD)
        key_parts += [key_high[own], key_low[own], key_high[own], bias8]
        query = jnp.concatenate([query_high[own], query_high[own], query_low[own], ones8], axis=0).astype(BF16)
        value_rows[h * 16 : (h + 1) * 16, :] = jnp.concatenate([values[own], ones8], axis=0).astype(BF16)
        for p in range(patches):
            query_rows[p * HEADS + h, h * 32 : (h + 1) * 32, :] = query[:, p * PATCH : (p + 1) * PATCH]
        alone = jnp.sum(scaled[own] * keys[own], axis=0, keepdims=True)
        self_rows[h] = jnp.where(live, AWAY, alone)
    key_parts.append(jnp.zeros((QROWS - HEADS * 32, rows), F32))
    key_rows[...] = jnp.concatenate(key_parts, axis=0).T.astype(BF16)

    def attend(p, h):
        cols = pl.ds(pl.multiple_of(p * PATCH, PATCH), PATCH)
        scores = dot(key_rows[cols, :], query_rows[p * HEADS + h])
        alone = self_rows[h, :, cols]
        largest = jnp.maximum(jnp.max(scores, axis=0, keepdims=True), alone)
        weights = jnp.exp2(scores - largest).astype(BF16)
        value = value_rows[pl.ds(pl.multiple_of(h * 16, 16), 16), cols]
        sums = dot(value, weights)
        own = jnp.exp2(alone - largest)
        top = sums[0:HD] + own * value[0:HD].astype(F32)
        heads_out[pl.ds(pl.multiple_of(h * HD, HD), HD), cols] = top / (sums[HD : HD + 1] + own)

    def attend_pair(i, _):
        p, h = i // (HEADS // 2), lax.rem(i, HEADS // 2) * 2
        attend(p, h)
        attend(p, h + 1)
        return 0

    lax.fori_loop(0, patches * HEADS // 2, attend_pair, 0)

    result = heads_out[...].astype(BF16)
    for g in range(nt // GROUP):
        back = dot(result, place[:, g * GROUP * cap : (g + 1) * GROUP * cap]).astype(BF16)
        for j in range(GROUP):
            k = g * GROUP + j
            part = back[:, j * cap : (j + 1) * cap]
            if k == 0:
                back_recv[0] = part
            else:
                back_send[k] = part
                back_copy(k).start()
    returned = None
    for g in range(nt // GROUP):
        for j in range(GROUP):
            if g + j:
                back_copy(g * GROUP + j).wait_recv()
        came = jnp.concatenate([back_recv[g * GROUP + j] for j in range(GROUP)], axis=1)
        part = dot(came, pack[g * GROUP * cap : (g + 1) * GROUP * cap, :])
        returned = part if g == 0 else returned + part
    attended = dot(w_out[...], returned.astype(BF16)).astype(BF16)
    gain = column_of(gain_mlp[...])
    for c in range(0, rows, 256):
        cols = slice(c, c + 256)
        combined = block_out[:, cols].astype(F32) + attended[:, cols].astype(F32)
        hidden = dot(w_up[...], normalise(combined, gain).astype(BF16))
        hidden = jax.nn.gelu(hidden).astype(BF16)
        summed = combined + dot(w_down[...], hidden)
        out_ref[:, cols] = jnp.where(occupied[:, cols], summed, 0.0).astype(BF16)

    for step in range(2):
        for o in range(4):
            halo_copy(step, o).wait_send()
    for k in range(1, nt):
        label_copy(k).wait_send()
        data_copy(k).wait_send()
        back_copy(k).wait_send()


def per_device(nb, nt, feats, occupancy, adjacency, serial_pos, conv_one, conv_two, gain_one, gain_two, gain_attn, w_qkv, w_out, gain_mlp, w_up, w_down):
    channels, rows = feats.shape
    slots = 2 * rows
    cap = slots // nt
    width = HEADS * HD
    vmem = pl.BlockSpec(memory_space=pltpu.VMEM)
    smem = pl.BlockSpec(memory_space=pltpu.SMEM)
    row = lambda x: x.reshape(1, -1)
    patches = rows // PATCH
    return pl.pallas_call(
        functools.partial(kernel, nb, nt),
        out_shape=jax.ShapeDtypeStruct((channels, rows), BF16),
        in_specs=[vmem, vmem, smem] + [vmem] * 11,
        out_specs=vmem,
        scratch_shapes=[
            pltpu.VMEM((channels, rows), BF16),
            pltpu.VMEM((7 * channels, rows), BF16),
            pltpu.VMEM((channels, 7 * channels), BF16),
            pltpu.VMEM((rows, 512), BF16),
            pltpu.VMEM((512, 768), BF16),
            pltpu.VMEM((rows, 768), BF16),
            pltpu.VMEM((2, 128, BLOCK), BF16),
            pltpu.VMEM((2, 4, channels, 128), BF16),
            pltpu.VMEM((2, 4, channels, 128), BF16),
            pltpu.VMEM((slots, rows), BF16),
            pltpu.VMEM((nt, 8, cap), F32),
            pltpu.VMEM((nt, 8, cap), F32),
            pltpu.VMEM((16, slots), BF16),
            pltpu.VMEM((rows, slots), BF16),
            pltpu.VMEM((channels, rows), BF16),
            pltpu.VMEM((nt, channels, cap), BF16),
            pltpu.VMEM((nt, channels, cap), BF16),
            pltpu.VMEM((channels + 16, rows), F32),
            pltpu.VMEM((rows, QROWS), BF16),
            pltpu.VMEM((patches * HEADS, QROWS, PATCH), BF16),
            pltpu.VMEM((HEADS * 16, rows), BF16),
            pltpu.VMEM((HEADS, 1, rows), F32),
            pltpu.VMEM((width, rows), F32),
            pltpu.VMEM((nt, width, cap), BF16),
            pltpu.VMEM((nt, width, cap), BF16),
            pltpu.SemaphoreType.DMA((2, 2, 4)),
            pltpu.SemaphoreType.DMA((2, nt)),
            pltpu.SemaphoreType.DMA((2, nt)),
            pltpu.SemaphoreType.DMA((2, nt)),
        ],
        compiler_params=pltpu.CompilerParams(collective_id=0, has_side_effects=True),
        name="voxel_step",
    )(
        feats,
        row(occupancy),
        adjacency,
        row(serial_pos),
        conv_one,
        conv_two,
        row(gain_one),
        row(gain_two),
        row(gain_attn),
        w_qkv,
        w_out,
        row(gain_mlp),
        w_up,
        w_down,
    )


def solution(mesh):
    nb, nt = mesh.shape["block"], mesh.shape["token"]
    split = ("block", "token")
    in_specs = (P(None, split), P(split), P(None, None, split), P(split)) + (P(),) * 10
    return jax.shard_map(
        functools.partial(per_device, nb, nt),
        mesh=mesh,
        in_specs=in_specs,
        out_specs=P(None, split),
        check_vma=False,
    )
```

```python
import functools
import math

import jax
import jax.numpy as jnp
from jax import lax
from jax.experimental import pallas as pl
from jax.experimental.pallas import tpu as pltpu
from jax.sharding import PartitionSpec as P

MESH = pl.DeviceIdType.MESH
F32 = jnp.float32
BF16 = jnp.bfloat16
I32 = jnp.int32

HEADS = 6
HD = 8
PATCH = 512
BLOCK = 512
FACE = 64
EPS = 1e-05
OFFS = (-2, -1, 1, 2)
SHIFTS = (64, -64, 8, -8, 1, -1)
AWAY = -1e30
NT_DIMS = (((1,), (1,)), ((), ()))
QROWS = 256
GROUP = 4
INPUTS = 14
RUNS = ((0, 3), (4, 5))
HEAD_ROWS = (slice(0, 32), slice(32, 48))
VMEM_LIMIT = 36 * 1024 * 1024


def dot(a, b):
    return jnp.dot(a, b, preferred_element_type=F32)


def dot_nt(a, b):
    return lax.dot_general(a, b, NT_DIMS, preferred_element_type=F32)


def face_index(face, place):
    high, low = place >> 3, place & 7
    if face == 0:
        return place
    if face == 1:
        return place + 448
    if face == 2:
        return high * 64 + low
    if face == 3:
        return high * 64 + low + 56
    if face == 4:
        return place * 8
    return place * 8 + 7


def store_one_hot(ref, row0, rows, lanes, index):
    width = index.shape[1]
    places = lax.broadcasted_iota(I32, (128, width), 0).astype(F32).astype(BF16)
    for part in range(rows // 128):
        here = jnp.where(index >> 7 == part, index & 127, -1).astype(F32).astype(BF16)
        hit = jnp.where(places == here, jnp.ones((), BF16), jnp.zeros((), BF16))
        ref[row0 + part * 128 : row0 + (part + 1) * 128, lanes] = hit


def column_of(row):
    size = row.shape[1]
    same = lax.broadcasted_iota(I32, (size, size), 0) == lax.broadcasted_iota(I32, (size, size), 1)
    return jnp.sum(jnp.where(same, row, 0.0), axis=1, keepdims=True)


def normalise(values, gain):
    center = values - jnp.mean(values, axis=0, keepdims=True)
    spread = jnp.mean(center * center, axis=0, keepdims=True)
    return center * lax.rsqrt(spread + EPS) * gain


def kernel(
    nb,
    nt,
    *refs,
):
    sources, out_ref, held = refs[:INPUTS], refs[INPUTS], refs[INPUTS + 1 : 2 * INPUTS + 1]
    (
        signal,
        taps,
        conv_cat,
        send_pick,
        remote_pick,
        local_pick,
        spread_pick,
        halo_send,
        halo_recv,
        pack,
        label_send,
        label_recv,
        live_rows,
        place,
        block_out,
        data_send,
        data_recv,
        serial_acc,
        key_rows,
        query_rows,
        value_rows,
        self_rows,
        heads_out,
        back_send,
        back_recv,
        halo_sems,
        label_sems,
        data_sems,
        back_sems,
        input_sems,
    ) = refs[2 * INPUTS + 1 :]
    loads = [pltpu.make_async_copy(sources[i], held[i], input_sems.at[i]) for i in range(INPUTS)]
    for load in loads:
        load.start()
    (
        feats,
        occupancy,
        adjacency,
        serial_pos,
        conv_one,
        conv_two,
        gain_one,
        gain_two,
        gain_attn,
        w_qkv,
        w_out,
        gain_mlp,
        w_up,
        w_down,
    ) = held
    channels, rows = feats.shape
    cap = pack.shape[0] // nt
    me_b = lax.axis_index("block")
    order = sorted(range(nt), key=lambda k: (-min(k, nt - k), k))
    me_t = lax.axis_index("token")

    barrier = pltpu.get_barrier_semaphore()
    for off in OFFS:
        pl.semaphore_signal(
            barrier, inc=1, device_id={"block": lax.rem(me_b + off + nb, nb)}, device_id_type=MESH
        )
    for k in range(1, nt):
        pl.semaphore_signal(
            barrier, inc=1, device_id={"token": lax.rem(me_t + k, nt)}, device_id_type=MESH
        )

    def halo_copy(step, o):
        return pltpu.make_async_remote_copy(
            src_ref=halo_send.at[step, o],
            dst_ref=halo_recv.at[step, o],
            send_sem=halo_sems.at[0, step, o],
            recv_sem=halo_sems.at[1, step, o],
            device_id={"block": lax.rem(me_b + OFFS[o] + nb, nb)},
            device_id_type=MESH,
        )

    def token_copy(source, target, sems, k, step):
        return pltpu.make_async_remote_copy(
            src_ref=source.at[k],
            dst_ref=target.at[k],
            send_sem=sems.at[0, k],
            recv_sem=sems.at[1, k],
            device_id={"token": lax.rem(me_t + step + nt, nt)},
            device_id_type=MESH,
        )

    label_copy = lambda k: token_copy(label_send, label_recv, label_sems, k, k)
    data_copy = lambda k: token_copy(data_send, data_recv, data_sems, k, k)

    def back_copy(t, k):
        return pltpu.make_async_remote_copy(
            src_ref=back_send.at[k, HEAD_ROWS[t]],
            dst_ref=back_recv.at[k, HEAD_ROWS[t]],
            send_sem=back_sems.at[0, t, k],
            recv_sem=back_sems.at[1, t, k],
            device_id={"token": lax.rem(me_t - k + nt, nt)},
            device_id_type=MESH,
        )


    for i in range(4):
        loads[i].wait()
    owner = {}
    index = {}
    for f in range(6):
        for b in range(2):
            owner[f, b] = adjacency[0, b, f]
            index[f, b] = adjacency[1, b, f]
    pairs = [(f, b) for f in range(6) for b in range(2)]
    lane = lax.broadcasted_iota(I32, (1, 128), 1)
    half, within = lane >> 6, lane & 63
    voxel_of = [face_index(f, within) for f in range(6)]
    for o, off in enumerate(OFFS):
        target = me_b + off
        count = jnp.int32(0)
        voxel = jnp.full((1, 128), -1, I32)
        for f, b in pairs:
            match = (owner[f, b] >= 0) & (owner[f, b] == target)
            slot = jnp.where(match, count, -1)
            count = count + jnp.where(match, 1, 0)
            voxel = jnp.where(half == slot, voxel_of[f] + b * BLOCK, voxel)
        store_one_hot(send_pick, 0, rows, slice(o * 128, (o + 1) * 128), voxel)

    occupied = occupancy[...] > 0
    field = jnp.where(occupied, feats[...].astype(F32), 0.0)
    signal[...] = field.astype(BF16)

    def send_halo(step):
        payload = dot(signal[...] if step == 0 else taps[0:channels, :], send_pick[...]).astype(BF16)
        for o in range(4):
            halo_send[step, o] = payload[:, o * 128 : (o + 1) * 128]

    send_halo(0)

    pl.semaphore_wait(barrier, 4 + nt - 1)

    for o in range(4):
        halo_copy(0, o).start()

    for a in range(3):
        for b in range(2):
            remote_src = jnp.full((1, 128), -1, I32)
            local_src = jnp.full((1, 128), -1, I32)
            for side in range(2):
                f = 2 * a + side
                own, idx = owner[f, b], index[f, b]
                key = (f ^ 1) * 2 + idx
                slot = jnp.int32(0)
                for f2, b2 in pairs:
                    if (f2, b2) != (f, b):
                        before = (owner[f2, b2] == own) & ((f2 ^ 1) * 2 + index[f2, b2] < key)
                        slot = slot + jnp.where(before, 1, 0)
                gap = me_b - own
                from_o = jnp.where(gap < 0, gap + 2, gap + 1)
                remote = (own >= 0) & (gap != 0)
                base = jnp.where(remote, from_o * 128 + slot * FACE, -4096)
                remote_src = jnp.where(half == side, within + base, remote_src)
                base = jnp.where((own >= 0) & (gap == 0), idx * BLOCK, -4096)
                local_src = jnp.where(half == side, voxel_of[f ^ 1] + base, local_src)
            lanes = slice((a * 2 + b) * 128, (a * 2 + b + 1) * 128)
            store_one_hot(remote_pick, 0, 512, lanes, remote_src)
            store_one_hot(local_pick, 0, rows, lanes, local_src)
    side_row = lax.broadcasted_iota(I32, (128, BLOCK), 0)
    voxel_lane = lax.broadcasted_iota(I32, (128, BLOCK), 1)
    for a in (1, 2):
        lower = face_index(2 * a, side_row & 63)
        upper = face_index(2 * a + 1, side_row & 63)
        hit = voxel_lane == jnp.where(side_row < 64, lower, upper)
        spread_pick[a - 1] = jnp.where(hit, 1.0, 0.0).astype(BF16)

    spot = lax.broadcasted_iota(I32, (1, rows), 1) & (BLOCK - 1)
    edges = [spot < 64, spot >= 448, (spot >> 3) & 7 == 0, (spot >> 3) & 7 == 7, spot & 7 == 0, spot & 7 == 7]
    on_edge = [jnp.where(e, 1.0, 0.0) for e in edges]

    def convolve(step, source, weight):
        for t in range(7):
            conv_cat[:, t * channels : (t + 1) * channels] = weight[t]
        for f in range(6):
            moved = pltpu.roll(source, SHIFTS[f] % rows, 1) * (1.0 - on_edge[f])
            taps[(f + 1) * channels : (f + 2) * channels, :] = moved.astype(BF16)
        halo = dot(taps[0:channels, :], local_pick[...])
        for o in range(4):
            halo_copy(step, o).wait_recv()
        received = jnp.concatenate([halo_recv[step, o] for o in range(4)], axis=1)
        halo = (halo + dot(received, remote_pick[...])).astype(BF16)
        for a in range(3):
            for b in range(2):
                lanes = slice((a * 2 + b) * 128, (a * 2 + b + 1) * 128)
                piece = halo[:, lanes]
                if a == 0:
                    gap = jnp.zeros((channels, BLOCK - 256), BF16)
                    wide = jnp.concatenate([piece, gap, piece], axis=1)
                else:
                    wide = dot(piece, spread_pick[a - 1]).astype(BF16)
                cols = slice(b * BLOCK, (b + 1) * BLOCK)
                for side in range(2):
                    f = 2 * a + side
                    tap_rows = slice((f + 1) * channels, (f + 2) * channels)
                    taps[tap_rows, cols] = taps[tap_rows, cols] + wide * on_edge[f][:, cols].astype(BF16)
        return dot(conv_cat[...], taps[...])

    for i in range(4, INPUTS):
        loads[i].wait()
    taps[0:channels, :] = signal[...]
    summed = convolve(0, field, conv_one)
    middle = jnp.where(occupied, jnp.maximum(normalise(summed, column_of(gain_one[...])), 0.0), 0.0)
    middle = middle.astype(BF16)
    taps[0:channels, :] = middle
    send_halo(1)
    for o in range(4):
        halo_copy(1, o).start()

    position = serial_pos[...]
    relative = ((position >> 10) - me_t + nt) & (nt - 1)
    sub16 = lax.broadcasted_iota(I32, (16, rows), 0)
    member = jnp.where(sub16 == relative, 1.0, 0.0)
    upto = lax.broadcasted_iota(I32, (128, 128), 0) <= lax.broadcasted_iota(I32, (128, 128), 1)
    upto = jnp.where(upto, 1.0, 0.0).astype(BF16)
    chunks = rows // 128
    stacked = jnp.concatenate(
        [member[:, c * 128 : (c + 1) * 128] for c in range(chunks)], axis=0
    ).astype(BF16)
    prefix = dot(stacked, upto)
    carry = jnp.zeros((16, 1), F32)
    ranks = []
    for c in range(chunks):
        piece = prefix[c * 16 : (c + 1) * 16, :]
        ranks.append(piece + carry - 1.0)
        carry = carry + piece[:, 127:128]
    slots = jnp.where(member > 0.5, jnp.concatenate(ranks, axis=1), -1.0).astype(I32)
    for k in range(nt):
        store_one_hot(pack, k * cap, cap, slice(0, rows), slots[k : k + 1, :])
    target_row = position & (rows - 1)
    facts = jnp.where(
        sub16 == 0,
        target_row >> 5,
        jnp.where(
            sub16 == 1,
            target_row & 31,
            jnp.where(sub16 == 2, jnp.where(occupied, 1, 0), jnp.where(sub16 == 3, 1, 0)),
        ),
    )
    facts = dot_nt(facts.astype(F32).astype(BF16), pack[...])
    goes_to = jnp.where(facts[3:4, :] > 0.5, facts[0:1, :] * 32.0 + facts[1:2, :], -1.0)
    sub8 = lax.broadcasted_iota(I32, (8, goes_to.shape[1]), 0)
    labels = jnp.where(sub8 == 0, goes_to, jnp.where(sub8 == 1, facts[2:3, :], 0.0))
    for k in range(nt):
        part = labels[:, k * cap : (k + 1) * cap]
        if k == 0:
            label_recv[0] = part
        else:
            label_send[k] = part

    for k in range(1, nt):
        label_copy(k).start()

    summed = convolve(1, middle.astype(F32), conv_two)
    result = jnp.maximum(signal[...].astype(F32) + normalise(summed, column_of(gain_two[...])), 0.0)
    result = jnp.where(occupied, result, 0.0).astype(BF16)
    block_out[...] = result
    normed = normalise(result.astype(F32), column_of(gain_attn[...])).astype(BF16)

    for g in range(nt // GROUP):
        ks = order[g * GROUP : (g + 1) * GROUP]
        chosen = jnp.concatenate([pack[k * cap : (k + 1) * cap, :] for k in ks], axis=0)
        packed = dot_nt(normed, chosen).astype(BF16)
        for j, k in enumerate(order[g * GROUP : (g + 1) * GROUP]):
            part = packed[:, j * cap : (j + 1) * cap]
            if k == 0:
                data_recv[0] = part
            else:
                data_send[k] = part
                data_copy(k).start()

    for k in range(1, nt):
        label_copy(k).wait_recv()
    for k in range(nt):
        label = label_recv[k]
        lanes = slice(k * cap, (k + 1) * cap)
        store_one_hot(place, 0, rows, lanes, label[0:1, :].astype(I32))
        live_rows[:, lanes] = jnp.broadcast_to(label[1:2, :], (16, cap)).astype(BF16)
    query_rows[...] = jnp.zeros_like(query_rows)
    w_out_here = w_out[...].astype(F32).T.astype(BF16)
    w_up_here = w_up[...].astype(F32).T.astype(BF16)
    for g in range(nt // GROUP):
        ks = order[g * GROUP : (g + 1) * GROUP]
        for k in ks:
            if k:
                data_copy(k).wait_recv()
        came = jnp.concatenate(
            [
                jnp.concatenate([data_recv[k], live_rows[:, k * cap : (k + 1) * cap]], axis=0)
                for k in ks
            ],
            axis=1,
        )
        chosen = jnp.concatenate([place[:, k * cap : (k + 1) * cap] for k in ks], axis=1)
        part = dot_nt(came, chosen)
        serial_acc[...] = part if g == 0 else serial_acc[...] + part

    live = serial_acc[channels : channels + 1, :] > 0.5
    width = HEADS * HD
    projected = dot(w_qkv[...], serial_acc[0:channels, :].astype(BF16))
    scaled = projected[:width, :] * (math.log2(math.e) / math.sqrt(HD))
    query_high = scaled.astype(BF16).astype(F32)
    query_low = scaled - query_high
    keys = projected[width : 2 * width, :]
    key_high = keys.astype(BF16).astype(F32)
    key_low = keys - key_high
    values = projected[2 * width :, :]
    sub8 = lax.broadcasted_iota(I32, (8, rows), 0)
    ones8 = jnp.where(sub8 == 0, 1.0, 0.0)
    bias8 = jnp.where((sub8 == 0) & jnp.logical_not(live), AWAY, 0.0)
    key_parts = []
    patches = rows // PATCH
    for h in range(HEADS):
        own = slice(h * HD, (h + 1) * HD)
        key_parts += [key_high[own], key_low[own], key_high[own], bias8]
        query = jnp.concatenate([query_high[own], query_high[own], query_low[own], ones8], axis=0).astype(BF16)
        value_rows[h * 16 : (h + 1) * 16, :] = jnp.concatenate([values[own], ones8], axis=0).astype(BF16)
        for p in range(patches):
            query_rows[p * HEADS + h, h * 32 : (h + 1) * 32, :] = query[:, p * PATCH : (p + 1) * PATCH]
        alone = jnp.sum(scaled[own] * keys[own], axis=0, keepdims=True)
        self_rows[h] = jnp.where(live, AWAY, alone)
    key_parts.append(jnp.zeros((QROWS - HEADS * 32, rows), F32))
    key_rows[...] = jnp.concatenate(key_parts, axis=0).T.astype(BF16)

    def score(p, h):
        return dot(key_rows[p * PATCH : (p + 1) * PATCH, :], query_rows[p * HEADS + h])

    def attend(p, h, scores):
        cols = slice(p * PATCH, (p + 1) * PATCH)
        alone = self_rows[h, :, cols]
        largest = jnp.maximum(jnp.max(scores, axis=0, keepdims=True), alone)
        weights = jnp.exp2(scores - largest).astype(BF16)
        value = value_rows[h * 16 : (h + 1) * 16, cols]
        sums = dot(value, weights)
        own = jnp.exp2(alone - largest)
        top = sums[0:HD] + own * value[0:HD].astype(F32)
        heads_out[h * HD : (h + 1) * HD, cols] = top / (sums[HD : HD + 1] + own)

    def to_slots(heads, p):
        part = heads_out[heads[0] * HD : (heads[1] + 1) * HD, p * PATCH : (p + 1) * PATCH].astype(BF16)
        return dot(part, place[p * PATCH : (p + 1) * PATCH, :])

    def give_back(t, slots):
        slots = slots.astype(BF16)
        for k in order:
            part = slots[:, k * cap : (k + 1) * cap]
            if k == 0:
                back_recv[0, HEAD_ROWS[t]] = part
            else:
                back_send[k, HEAD_ROWS[t]] = part
        for k in order:
            if k:
                back_copy(t, k).start()

    waves = [(t, p) for t in range(len(RUNS)) for p in range(patches)]
    units = [(t, p, h) for t, p in waves for h in range(RUNS[t][0], RUNS[t][1] + 1)]
    ahead = score(*units[0][1:])
    slots = None
    for i, (t, p, h) in enumerate(units):
        scores = ahead
        if i + 1 < len(units):
            ahead = score(*units[i + 1][1:])
        attend(p, h, scores)
        if h == RUNS[t][1]:
            part = to_slots(RUNS[t], p)
            slots = part if p == 0 else slots + part
            if p == patches - 1:
                give_back(t, slots)

    returned = None
    for g in range(nt // GROUP):
        ks = order[g * GROUP : (g + 1) * GROUP]
        for k in ks:
            if k:
                for t in range(len(RUNS)):
                    back_copy(t, k).wait_recv()
        came = jnp.concatenate([back_recv[k] for k in ks], axis=1)
        part = dot(came, jnp.concatenate([pack[k * cap : (k + 1) * cap, :] for k in ks], axis=0))
        returned = part if g == 0 else returned + part
    attended = dot(w_out_here, returned.astype(BF16)).astype(BF16)
    gain = column_of(gain_mlp[...])
    for c in range(0, rows, 256):
        cols = slice(c, c + 256)
        combined = block_out[:, cols].astype(F32) + attended[:, cols].astype(F32)
        hidden = dot(w_up_here, normalise(combined, gain).astype(BF16))
        hidden = jax.nn.gelu(hidden).astype(BF16)
        summed = combined + dot(w_down[...], hidden)
        out_ref[:, cols] = jnp.where(occupied[:, cols], summed, 0.0).astype(BF16)

    for step in range(2):
        for o in range(4):
            halo_copy(step, o).wait_send()
    for k in range(1, nt):
        label_copy(k).wait_send()
        data_copy(k).wait_send()
        for t in range(len(RUNS)):
            back_copy(t, k).wait_send()


def per_device(nb, nt, feats, occupancy, adjacency, serial_pos, conv_one, conv_two, gain_one, gain_two, gain_attn, w_qkv, w_out, gain_mlp, w_up, w_down):
    channels, rows = feats.shape
    slots = 2 * rows
    cap = slots // nt
    width = HEADS * HD
    row = lambda x: x.reshape(1, -1)
    patches = rows // PATCH
    inputs = (
        feats,
        row(occupancy),
        adjacency.transpose(0, 2, 1),
        row(serial_pos),
        conv_one,
        conv_two,
        row(gain_one),
        row(gain_two),
        row(gain_attn),
        w_qkv,
        w_out.T,
        row(gain_mlp),
        w_up.T,
        w_down,
    )
    return pl.pallas_call(
        functools.partial(kernel, nb, nt),
        out_shape=jax.ShapeDtypeStruct((channels, rows), BF16),
        in_specs=[pl.BlockSpec(memory_space=pltpu.HBM)] * INPUTS,
        out_specs=pl.BlockSpec(memory_space=pltpu.VMEM),
        scratch_shapes=[
            pltpu.SMEM(x.shape, x.dtype) if i == 2 else pltpu.VMEM(x.shape, x.dtype)
            for i, x in enumerate(inputs)
        ]
        + [
            pltpu.VMEM((channels, rows), BF16),
            pltpu.VMEM((7 * channels, rows), BF16),
            pltpu.VMEM((channels, 7 * channels), BF16),
            pltpu.VMEM((rows, 512), BF16),
            pltpu.VMEM((512, 768), BF16),
            pltpu.VMEM((rows, 768), BF16),
            pltpu.VMEM((2, 128, BLOCK), BF16),
            pltpu.VMEM((2, 4, channels, 128), BF16),
            pltpu.VMEM((2, 4, channels, 128), BF16),
            pltpu.VMEM((slots, rows), BF16),
            pltpu.VMEM((nt, 8, cap), F32),
            pltpu.VMEM((nt, 8, cap), F32),
            pltpu.VMEM((16, slots), BF16),
            pltpu.VMEM((rows, slots), BF16),
            pltpu.VMEM((channels, rows), BF16),
            pltpu.VMEM((nt, channels, cap), BF16),
            pltpu.VMEM((nt, channels, cap), BF16),
            pltpu.VMEM((channels + 16, rows), F32),
            pltpu.VMEM((rows, QROWS), BF16),
            pltpu.VMEM((patches * HEADS, QROWS, PATCH), BF16),
            pltpu.VMEM((HEADS * 16, rows), BF16),
            pltpu.VMEM((HEADS, 1, rows), F32),
            pltpu.VMEM((width, rows), F32),
            pltpu.VMEM((nt, width, cap), BF16),
            pltpu.VMEM((nt, width, cap), BF16),
            pltpu.SemaphoreType.DMA((2, 2, 4)),
            pltpu.SemaphoreType.DMA((2, nt)),
            pltpu.SemaphoreType.DMA((2, nt)),
            pltpu.SemaphoreType.DMA((2, len(RUNS), nt)),
            pltpu.SemaphoreType.DMA((INPUTS,)),
        ],
        compiler_params=pltpu.CompilerParams(
            collective_id=0, has_side_effects=True, vmem_limit_bytes=VMEM_LIMIT
        ),
        name="voxel_step",
    )(*[pltpu.with_memory_space_constraint(x, pltpu.HBM) for x in inputs])


def solution(mesh):
    nb, nt = mesh.shape["block"], mesh.shape["token"]
    split = ("block", "token")
    in_specs = (P(None, split), P(split), P(None, None, split), P(split)) + (P(),) * 10
    return jax.shard_map(
        functools.partial(per_device, nb, nt),
        mesh=mesh,
        in_specs=in_specs,
        out_specs=P(None, split),
        check_vma=False,
    )
```

```python
import functools
import math

import jax
import jax.numpy as jnp
from jax import lax
from jax.experimental import pallas as pl
from jax.experimental.pallas import tpu as pltpu
from jax.sharding import PartitionSpec as P

MESH = pl.DeviceIdType.MESH
F32 = jnp.float32
BF16 = jnp.bfloat16
I32 = jnp.int32

HEADS = 6
HD = 8
PATCH = 512
BLOCK = 512
FACE = 64
EPS = 1e-05
OFFS = (-2, -1, 1, 2)
SHIFTS = (64, -64, 8, -8, 1, -1)
AWAY = -1e30
NT_DIMS = (((1,), (1,)), ((), ()))
SET = 4
GROUP = 4
INPUTS = 14
WAVES = ((0, 1, 2, 3), (4, 5))
WAVE_ROWS = (slice(0, 32), slice(32, 48))
GELU_ONE = math.sqrt(2 / math.pi)
GELU_THREE = GELU_ONE * 0.044715
VMEM_LIMIT = 36 * 1024 * 1024


def dot(a, b):
    return jnp.dot(a, b, preferred_element_type=F32)


def dot_nt(a, b):
    return lax.dot_general(a, b, NT_DIMS, preferred_element_type=F32)


def face_index(face, place):
    high, low = place >> 3, place & 7
    if face == 0:
        return place
    if face == 1:
        return place + 448
    if face == 2:
        return high * 64 + low
    if face == 3:
        return high * 64 + low + 56
    if face == 4:
        return place * 8
    return place * 8 + 7


def store_one_hot(ref, row0, rows, lanes, index):
    width = index.shape[1]
    places = lax.broadcasted_iota(I32, (128, width), 0).astype(F32).astype(BF16)
    for part in range(rows // 128):
        here = jnp.where(index >> 7 == part, index & 127, -1).astype(F32).astype(BF16)
        hit = jnp.where(places == here, jnp.ones((), BF16), jnp.zeros((), BF16))
        ref[row0 + part * 128 : row0 + (part + 1) * 128, lanes] = hit


def column_of(row):
    size = row.shape[1]
    same = lax.broadcasted_iota(I32, (size, size), 0) == lax.broadcasted_iota(I32, (size, size), 1)
    return jnp.sum(jnp.where(same, row, 0.0), axis=1, keepdims=True)


def normalise(values, gain):
    center = values - jnp.mean(values, axis=0, keepdims=True)
    spread = jnp.mean(center * center, axis=0, keepdims=True)
    return center * lax.rsqrt(spread + EPS) * gain


def kernel(
    nb,
    nt,
    *refs,
):
    sources, out_ref, held = refs[:INPUTS], refs[INPUTS], refs[INPUTS + 1 : 2 * INPUTS + 1]
    (
        signal,
        taps,
        conv_cat,
        inside,
        send_pick,
        local_pick,
        spread_pick,
        halo_send,
        halo_recv,
        pack,
        label_send,
        label_recv,
        live_rows,
        place,
        block_out,
        data_send,
        data_recv,
        serial_acc,
        key_rows,
        query_rows,
        value_rows,
        self_rows,
        heads_out,
        slot_acc,
        back_send,
        back_recv,
        halo_sems,
        label_sems,
        data_sems,
        back_sems,
        input_sems,
    ) = refs[2 * INPUTS + 1 :]
    loads = [pltpu.make_async_copy(sources[i], held[i], input_sems.at[i]) for i in range(INPUTS)]
    (
        feats,
        occupancy,
        adjacency,
        serial_pos,
        conv_one,
        conv_two,
        gain_one,
        gain_two,
        gain_attn,
        w_qkv,
        w_out,
        gain_mlp,
        w_up,
        w_down,
    ) = held
    channels, rows = feats.shape
    cap = pack.shape[0] // nt
    me_b = lax.axis_index("block")
    order = sorted(range(nt), key=lambda k: (-min(k, nt - k), k))
    me_t = lax.axis_index("token")

    barrier = pltpu.get_barrier_semaphore()
    for off in OFFS:
        pl.semaphore_signal(
            barrier, inc=1, device_id={"block": lax.rem(me_b + off + nb, nb)}, device_id_type=MESH
        )
    for load in loads:
        load.start()
    for k in range(1, nt):
        pl.semaphore_signal(
            barrier, inc=1, device_id={"token": lax.rem(me_t + k, nt)}, device_id_type=MESH
        )

    def halo_copy(step, o):
        return pltpu.make_async_remote_copy(
            src_ref=halo_send.at[step, o],
            dst_ref=halo_recv.at[step, o],
            send_sem=halo_sems.at[0, step, o],
            recv_sem=halo_sems.at[1, step, o],
            device_id={"block": lax.rem(me_b + OFFS[o] + nb, nb)},
            device_id_type=MESH,
        )

    def token_copy(source, target, sems, k, step):
        return pltpu.make_async_remote_copy(
            src_ref=source.at[k],
            dst_ref=target.at[k],
            send_sem=sems.at[0, k],
            recv_sem=sems.at[1, k],
            device_id={"token": lax.rem(me_t + step + nt, nt)},
            device_id_type=MESH,
        )

    label_copy = lambda k: token_copy(label_send, label_recv, label_sems, k, k)
    data_copy = lambda k: token_copy(data_send, data_recv, data_sems, k, k)


    def back_copy(wave, k):
        return pltpu.make_async_remote_copy(
            src_ref=back_send.at[k, WAVE_ROWS[wave]],
            dst_ref=back_recv.at[k, WAVE_ROWS[wave]],
            send_sem=back_sems.at[0, wave, k],
            recv_sem=back_sems.at[1, wave, k],
            device_id={"token": lax.rem(me_t - k + nt, nt)},
            device_id_type=MESH,
        )

    for i in range(4):
        loads[i].wait()
    owner = {}
    index = {}
    for f in range(6):
        for b in range(2):
            owner[f, b] = adjacency[0, b, f]
            index[f, b] = adjacency[1, b, f]
    pairs = [(f, b) for f in range(6) for b in range(2)]
    lane = lax.broadcasted_iota(I32, (1, 128), 1)
    half, within = lane >> 6, lane & 63
    voxel_of = [face_index(f, within) for f in range(6)]
    for o, off in enumerate(OFFS):
        target = me_b + off
        count = jnp.int32(0)
        voxel = jnp.full((1, 128), -1, I32)
        for f, b in pairs:
            match = (owner[f, b] >= 0) & (owner[f, b] == target)
            slot = jnp.where(match, count, -1)
            count = count + jnp.where(match, 1, 0)
            voxel = jnp.where(half == slot, voxel_of[f] + b * BLOCK, voxel)
        store_one_hot(send_pick, 0, rows, slice(o * 128, (o + 1) * 128), voxel)

    occupied = occupancy[...] > 0
    field = jnp.where(occupied, feats[...].astype(F32), 0.0)
    signal[...] = field.astype(BF16)

    def send_halo(step):
        payload = dot(signal[...] if step == 0 else taps[0:channels, :], send_pick[...]).astype(BF16)
        for o in range(4):
            halo_send[step, o] = payload[:, o * 128 : (o + 1) * 128]

    send_halo(0)

    pl.semaphore_wait(barrier, 4 + nt - 1)

    for o in range(4):
        halo_copy(0, o).start()

    takes = {}
    for a in range(3):
        for b in range(2):
            local_src = jnp.full((1, 128), -1, I32)
            source_of = []
            for side in range(2):
                f = 2 * a + side
                own, idx = owner[f, b], index[f, b]
                key = (f ^ 1) * 2 + idx
                slot = jnp.int32(0)
                for f2, b2 in pairs:
                    if (f2, b2) != (f, b):
                        before = (owner[f2, b2] == own) & ((f2 ^ 1) * 2 + index[f2, b2] < key)
                        slot = slot + jnp.where(before, 1, 0)
                gap = me_b - own
                from_o = jnp.where(gap < 0, gap + 2, gap + 1)
                source_of.append(jnp.where((own >= 0) & (gap != 0), from_o * 2 + slot, -1))
                base = jnp.where((own >= 0) & (gap == 0), idx * BLOCK, -4096)
                local_src = jnp.where(half == side, voxel_of[f ^ 1] + base, local_src)
            source = jnp.where(half == 0, source_of[0], source_of[1])
            for o in range(4):
                for cross in range(2):
                    hit = source == o * 2 + (half ^ cross)
                    takes[a, b, o, cross] = jnp.where(hit, 1.0, 0.0).astype(BF16)
            lanes = slice((a * 2 + b) * 128, (a * 2 + b + 1) * 128)
            store_one_hot(local_pick, 0, rows, lanes, local_src)
    side_row = lax.broadcasted_iota(I32, (128, BLOCK), 0)
    voxel_lane = lax.broadcasted_iota(I32, (128, BLOCK), 1)
    for a in (1, 2):
        lower = face_index(2 * a, side_row & 63)
        upper = face_index(2 * a + 1, side_row & 63)
        hit = voxel_lane == jnp.where(side_row < 64, lower, upper)
        spread_pick[a - 1] = jnp.where(hit, 1.0, 0.0).astype(BF16)

    spot = lax.broadcasted_iota(I32, (1, rows), 1) & (BLOCK - 1)
    edges = [spot < 64, spot >= 448, (spot >> 3) & 7 == 0, (spot >> 3) & 7 == 7, spot & 7 == 0, spot & 7 == 7]
    on_edge = [jnp.where(e, 1.0, 0.0) for e in edges]

    def convolve(step, source, weight):
        for t in range(7):
            conv_cat[:, t * channels : (t + 1) * channels] = weight[t]
        for f in range(6):
            moved = pltpu.roll(source, SHIFTS[f] % rows, 1) * (1.0 - on_edge[f])
            taps[(f + 1) * channels : (f + 2) * channels, :] = moved.astype(BF16)
        local = dot(taps[0:channels, :], local_pick[...]).astype(BF16)
        inside[...] = dot(conv_cat[...], taps[...])
        for o in range(4):
            halo_copy(step, o).wait_recv()
        came = [halo_recv[step, o] for o in range(4)]
        came = [(x, jnp.concatenate([x[:, FACE:], x[:, :FACE]], axis=1)) for x in came]

        def faces(a, b):
            piece = local[:, (a * 2 + b) * 128 : (a * 2 + b + 1) * 128]
            for o in range(4):
                for cross in range(2):
                    piece = piece + came[o][cross] * takes[a, b, o, cross]
            return piece

        tiles = [inside[:, c * 128 : (c + 1) * 128] for c in range(rows // 128)]
        per_block = BLOCK // 128
        for a in range(3):
            pair = weight[2 * a + 1 : 2 * a + 3].reshape(2 * channels, channels)
            sides = dot(pair, jnp.concatenate([faces(a, 0), faces(a, 1)], axis=1))
            edge = [
                jnp.where(half == 0, sides[:channels, lanes], sides[channels:, lanes])
                for lanes in (slice(0, 128), slice(128, 256))
            ]
            if a == 0:
                for b in range(2):
                    first, last = b * per_block, (b + 1) * per_block - 1
                    tiles[first] = tiles[first] + jnp.where(half == 0, edge[b], 0.0)
                    tiles[last] = tiles[last] + jnp.where(half == 1, edge[b], 0.0)
            else:
                high = [e.astype(BF16) for e in edge]
                low = [(e - h.astype(F32)).astype(BF16) for e, h in zip(edge, high)]
                wide = dot(jnp.concatenate(high + low, axis=0), spread_pick[a - 1])
                for b in range(2):
                    part = wide[b * channels : (b + 1) * channels] + wide[(b + 2) * channels : (b + 3) * channels]
                    for c in range(per_block):
                        t = b * per_block + c
                        tiles[t] = tiles[t] + part[:, c * 128 : (c + 1) * 128]
        return jnp.concatenate(tiles, axis=1)

    for i in range(4, INPUTS):
        loads[i].wait()
    taps[0:channels, :] = signal[...]
    summed = convolve(0, field, conv_one)
    middle = jnp.where(occupied, jnp.maximum(normalise(summed, column_of(gain_one[...])), 0.0), 0.0)
    middle = middle.astype(BF16)
    taps[0:channels, :] = middle
    send_halo(1)
    for o in range(4):
        halo_copy(1, o).start()

    position = serial_pos[...]
    relative = ((position >> 10) - me_t + nt) & (nt - 1)
    sub16 = lax.broadcasted_iota(I32, (16, rows), 0)
    member = jnp.where(sub16 == relative, 1.0, 0.0)
    upto = lax.broadcasted_iota(I32, (128, 128), 0) <= lax.broadcasted_iota(I32, (128, 128), 1)
    upto = jnp.where(upto, 1.0, 0.0).astype(BF16)
    chunks = rows // 128
    stacked = jnp.concatenate(
        [member[:, c * 128 : (c + 1) * 128] for c in range(chunks)], axis=0
    ).astype(BF16)
    prefix = dot(stacked, upto)
    carry = jnp.zeros((16, 1), F32)
    ranks = []
    for c in range(chunks):
        piece = prefix[c * 16 : (c + 1) * 16, :]
        ranks.append(piece + carry - 1.0)
        carry = carry + piece[:, 127:128]
    slots = jnp.where(member > 0.5, jnp.concatenate(ranks, axis=1), -1.0).astype(I32)
    for k in range(nt):
        store_one_hot(pack, k * cap, cap, slice(0, rows), slots[k : k + 1, :])
    target_row = position & (rows - 1)
    facts = jnp.where(
        sub16 == 0,
        target_row >> 5,
        jnp.where(
            sub16 == 1,
            target_row & 31,
            jnp.where(sub16 == 2, jnp.where(occupied, 1, 0), jnp.where(sub16 == 3, 1, 0)),
        ),
    )
    facts = dot_nt(facts.astype(F32).astype(BF16), pack[...])
    goes_to = jnp.where(facts[3:4, :] > 0.5, facts[0:1, :] * 32.0 + facts[1:2, :], -1.0)
    sub8 = lax.broadcasted_iota(I32, (8, goes_to.shape[1]), 0)
    labels = jnp.where(sub8 == 0, goes_to, jnp.where(sub8 == 1, facts[2:3, :], 0.0))
    for k in range(nt):
        part = labels[:, k * cap : (k + 1) * cap]
        if k == 0:
            label_recv[0] = part
        else:
            label_send[k] = part

    for k in range(1, nt):
        label_copy(k).start()

    summed = convolve(1, middle.astype(F32), conv_two)
    result = jnp.maximum(signal[...].astype(F32) + normalise(summed, column_of(gain_two[...])), 0.0)
    result = jnp.where(occupied, result, 0.0).astype(BF16)
    block_out[...] = result
    normed = normalise(result.astype(F32), column_of(gain_attn[...])).astype(BF16)

    for ks in [order[:2], order[2:4]] + [order[g : g + GROUP] for g in range(4, nt, GROUP)]:
        chosen = jnp.concatenate([pack[k * cap : (k + 1) * cap, :] for k in ks], axis=0)
        packed = dot_nt(normed, chosen).astype(BF16)
        for j, k in enumerate(ks):
            part = packed[:, j * cap : (j + 1) * cap]
            if k == 0:
                data_recv[0] = part
            else:
                data_send[k] = part
                data_copy(k).start()

    for k in range(1, nt):
        label_copy(k).wait_recv()
    for k in range(nt):
        label = label_recv[k]
        lanes = slice(k * cap, (k + 1) * cap)
        store_one_hot(place, 0, rows, lanes, label[0:1, :].astype(I32))
        live_rows[:, lanes] = jnp.broadcast_to(label[1:2, :], (16, cap)).astype(BF16)
    query_rows[...] = jnp.zeros_like(query_rows)
    w_out_here = w_out[...].astype(F32).T.astype(BF16)
    w_up_here = w_up[...].astype(F32).T.astype(BF16)
    arrivals = [order[g : g + GROUP] for g in range(0, nt - GROUP, GROUP)] + [order[-GROUP:-2], order[-2:]]
    for g, ks in enumerate(arrivals):
        for k in ks:
            if k:
                data_copy(k).wait_recv()
        came = jnp.concatenate(
            [
                jnp.concatenate([data_recv[k], live_rows[:, k * cap : (k + 1) * cap]], axis=0)
                for k in ks
            ],
            axis=1,
        )
        chosen = jnp.concatenate([place[:, k * cap : (k + 1) * cap] for k in ks], axis=1)
        part = dot_nt(came, chosen)
        serial_acc[...] = part if g == 0 else serial_acc[...] + part

    groups = [order[g * GROUP : (g + 1) * GROUP] for g in range(nt // GROUP)]
    live = serial_acc[channels : channels + 1, :] > 0.5
    width = HEADS * HD
    projected = dot(w_qkv[...], serial_acc[0:channels, :].astype(BF16))
    scaled = projected[:width, :] * (math.log2(math.e) / math.sqrt(HD))
    query_high = scaled.astype(BF16).astype(F32)
    query_low = scaled - query_high
    keys = projected[width : 2 * width, :]
    key_high = keys.astype(BF16).astype(F32)
    key_low = keys - key_high
    values = projected[2 * width :, :]
    sub8 = lax.broadcasted_iota(I32, (8, rows), 0)
    ones8 = jnp.where(sub8 == 0, 1.0, 0.0)
    bias8 = jnp.where((sub8 == 0) & jnp.logical_not(live), AWAY, 0.0)
    key_parts = []
    patches = rows // PATCH
    for h in range(HEADS):
        own = slice(h * HD, (h + 1) * HD)
        key_parts += [key_high[own], key_low[own], key_high[own], bias8]
        query = jnp.concatenate([query_high[own], query_high[own], query_low[own], ones8], axis=0).astype(BF16)
        value_rows[h * 16 : (h + 1) * 16, :] = jnp.concatenate([values[own], ones8], axis=0).astype(BF16)
        for p in range(patches):
            query_rows[p * HEADS + h, h % SET * 32 : (h % SET + 1) * 32, :] = query[:, p * PATCH : (p + 1) * PATCH]
        alone = jnp.sum(scaled[own] * keys[own], axis=0, keepdims=True)
        self_rows[h] = jnp.where(live, AWAY, alone)
    key_rows[...] = jnp.concatenate(key_parts, axis=0).astype(BF16).T

    def score(p, h):
        first = h // SET * SET
        last = min(first + SET, HEADS)
        return dot(
            key_rows[p * PATCH : (p + 1) * PATCH, first * 32 : last * 32],
            query_rows[p * HEADS + h, 0 : (last - first) * 32],
        )

    def attend(p, h, scores):
        cols = slice(p * PATCH, (p + 1) * PATCH)
        alone = self_rows[h, :, cols]
        largest = jnp.maximum(jnp.max(scores, axis=0, keepdims=True), alone)
        weights = jnp.exp2(scores - largest).astype(BF16)
        value = value_rows[h * 16 : (h + 1) * 16, cols]
        sums = dot(value, weights)
        own = jnp.exp2(alone - largest)
        top = sums[0:HD] + own * value[0:HD].astype(F32)
        heads_out[h * HD : (h + 1) * HD, cols] = top / (sums[HD : HD + 1] + own)

    def to_slots(wave, p, ks):
        heads = WAVES[wave]
        part = heads_out[heads[0] * HD : (heads[-1] + 1) * HD, p * PATCH : (p + 1) * PATCH].astype(BF16)
        chosen = [place[p * PATCH : (p + 1) * PATCH, k * cap : (k + 1) * cap] for k in ks]
        return dot(part, jnp.concatenate(chosen, axis=1))

    def add_slots(wave, p):
        for g, ks in enumerate(groups):
            part = to_slots(wave, p, ks)
            slot_acc[g, WAVE_ROWS[wave]] = part if p == 0 else slot_acc[g, WAVE_ROWS[wave]] + part

    def give_back(wave, last):
        for g, ks in enumerate(groups):
            back = slot_acc[g, WAVE_ROWS[wave]]
            if last:
                back = back + to_slots(wave, patches - 1, ks)
            back = back.astype(BF16)
            for j, k in enumerate(ks):
                part = back[:, j * cap : (j + 1) * cap]
                if k == 0:
                    back_recv[0, WAVE_ROWS[wave]] = part
                else:
                    back_send[k, WAVE_ROWS[wave]] = part
                    if last:
                        back_copy(wave, k).start()
        if not last:
            for k in order:
                if k:
                    back_copy(wave, k).start()

    units = [(wave, p, h) for wave in range(2) for p in range(patches) for h in WAVES[wave]]
    ahead = score(*units[0][1:])
    waiting = []
    for i, (wave, p, h) in enumerate(units):
        scores = ahead
        if i + 1 < len(units):
            ahead = score(*units[i + 1][1:])
        attend(p, h, scores)
        if waiting and h == WAVES[wave][0]:
            done = waiting.pop()
            add_slots(*done)
            if done == (0, patches - 1):
                give_back(0, False)
        if h == WAVES[wave][-1]:
            waiting.append((wave, p))
    give_back(1, True)

    returned = None
    for g in range(nt // GROUP):
        ks = order[g * GROUP : (g + 1) * GROUP]
        for k in ks:
            if k:
                for wave in range(2):
                    back_copy(wave, k).wait_recv()
        came = jnp.concatenate([back_recv[k] for k in ks], axis=1)
        part = dot(came, jnp.concatenate([pack[k * cap : (k + 1) * cap, :] for k in ks], axis=0))
        returned = part if g == 0 else returned + part
    attended = dot(w_out_here, returned.astype(BF16)).astype(BF16)
    gain = column_of(gain_mlp[...])
    for c in range(0, rows, 256):
        cols = slice(c, c + 256)
        combined = block_out[:, cols].astype(F32) + attended[:, cols].astype(F32)
        hidden = dot(w_up_here, normalise(combined, gain).astype(BF16))
        inner = hidden * (GELU_ONE + GELU_THREE * (hidden * hidden))
        hidden = (hidden + hidden * jnp.tanh(inner)).astype(BF16)
        summed = combined + 0.5 * dot(w_down[...], hidden)
        out_ref[:, cols] = jnp.where(occupied[:, cols], summed, 0.0).astype(BF16)

    for step in range(2):
        for o in range(4):
            halo_copy(step, o).wait_send()
    for k in range(1, nt):
        label_copy(k).wait_send()
        data_copy(k).wait_send()
        for wave in range(2):
            back_copy(wave, k).wait_send()


def per_device(nb, nt, feats, occupancy, adjacency, serial_pos, conv_one, conv_two, gain_one, gain_two, gain_attn, w_qkv, w_out, gain_mlp, w_up, w_down):
    channels, rows = feats.shape
    slots = 2 * rows
    cap = slots // nt
    width = HEADS * HD
    row = lambda x: x.reshape(1, -1)
    patches = rows // PATCH
    inputs = (
        feats,
        row(occupancy),
        adjacency.transpose(0, 2, 1),
        row(serial_pos),
        conv_one,
        conv_two,
        row(gain_one),
        row(gain_two),
        row(gain_attn),
        w_qkv,
        w_out.T,
        row(gain_mlp),
        w_up.T,
        w_down,
    )
    return pl.pallas_call(
        functools.partial(kernel, nb, nt),
        out_shape=jax.ShapeDtypeStruct((channels, rows), BF16),
        in_specs=[pl.BlockSpec(memory_space=pltpu.HBM)] * INPUTS,
        out_specs=pl.BlockSpec(memory_space=pltpu.VMEM),
        scratch_shapes=[
            pltpu.SMEM(x.shape, x.dtype) if i == 2 else pltpu.VMEM(x.shape, x.dtype)
            for i, x in enumerate(inputs)
        ]
        + [
            pltpu.VMEM((channels, rows), BF16),
            pltpu.VMEM((7 * channels, rows), BF16),
            pltpu.VMEM((channels, 7 * channels), BF16),
            pltpu.VMEM((channels, rows), F32),
            pltpu.VMEM((rows, 512), BF16),
            pltpu.VMEM((rows, 768), BF16),
            pltpu.VMEM((2, 128, BLOCK), BF16),
            pltpu.VMEM((2, 4, channels, 128), BF16),
            pltpu.VMEM((2, 4, channels, 128), BF16),
            pltpu.VMEM((slots, rows), BF16),
            pltpu.VMEM((nt, 8, cap), F32),
            pltpu.VMEM((nt, 8, cap), F32),
            pltpu.VMEM((16, slots), BF16),
            pltpu.VMEM((rows, slots), BF16),
            pltpu.VMEM((channels, rows), BF16),
            pltpu.VMEM((nt, channels, cap), BF16),
            pltpu.VMEM((nt, channels, cap), BF16),
            pltpu.VMEM((channels + 16, rows), F32),
            pltpu.VMEM((rows, HEADS * 32), BF16),
            pltpu.VMEM((patches * HEADS, SET * 32, PATCH), BF16),
            pltpu.VMEM((HEADS * 16, rows), BF16),
            pltpu.VMEM((HEADS, 1, rows), F32),
            pltpu.VMEM((width, rows), F32),
            pltpu.VMEM((nt // GROUP, width, GROUP * cap), F32),
            pltpu.VMEM((nt, width, cap), BF16),
            pltpu.VMEM((nt, width, cap), BF16),
            pltpu.SemaphoreType.DMA((2, 2, 4)),
            pltpu.SemaphoreType.DMA((2, nt)),
            pltpu.SemaphoreType.DMA((2, nt)),
            pltpu.SemaphoreType.DMA((2, 2, nt)),
            pltpu.SemaphoreType.DMA((INPUTS,)),
        ],
        compiler_params=pltpu.CompilerParams(
            collective_id=0, has_side_effects=True, vmem_limit_bytes=VMEM_LIMIT
        ),
        name="voxel_step",
    )(*[pltpu.with_memory_space_constraint(x, pltpu.HBM) for x in inputs])


def solution(mesh):
    nb, nt = mesh.shape["block"], mesh.shape["token"]
    split = ("block", "token")
    in_specs = (P(None, split), P(split), P(None, None, split), P(split)) + (P(),) * 10
    return jax.shard_map(
        functools.partial(per_device, nb, nt),
        mesh=mesh,
        in_specs=in_specs,
        out_specs=P(None, split),
        check_vma=False,
    )
```

```python
import functools
import math

import jax
import jax.numpy as jnp
from jax import lax
from jax.experimental import pallas as pl
from jax.experimental.pallas import tpu as pltpu
from jax.sharding import PartitionSpec as P

MESH = pl.DeviceIdType.MESH
F32 = jnp.float32
BF16 = jnp.bfloat16
I32 = jnp.int32

HEADS = 6
HD = 8
PATCH = 512
BLOCK = 512
FACE = 64
EPS = 1e-05
OFFS = (-2, -1, 1, 2)
SHIFTS = (64, -64, 8, -8, 1, -1)
AWAY = -1e30
NT_DIMS = (((1,), (1,)), ((), ()))
SET = 4
QCOLS = 256
GROUP = 4
INPUTS = 14
WAVES = ((0, 1, 2, 3), (4, 5))
WAVE_ROWS = (slice(0, 32), slice(32, 48))
GELU_ONE = math.sqrt(2 / math.pi)
GELU_THREE = GELU_ONE * 0.044715
VMEM_LIMIT = 36 * 1024 * 1024


def dot(a, b):
    return jnp.dot(a, b, preferred_element_type=F32)


def dot_nt(a, b):
    return lax.dot_general(a, b, NT_DIMS, preferred_element_type=F32)


def face_index(face, place):
    high, low = place >> 3, place & 7
    if face == 0:
        return place
    if face == 1:
        return place + 448
    if face == 2:
        return high * 64 + low
    if face == 3:
        return high * 64 + low + 56
    if face == 4:
        return place * 8
    return place * 8 + 7


def store_one_hot(ref, row0, rows, lanes, index):
    width = index.shape[1]
    places = lax.broadcasted_iota(I32, (128, width), 0).astype(F32).astype(BF16)
    for part in range(rows // 128):
        here = jnp.where(index >> 7 == part, index & 127, -1).astype(F32).astype(BF16)
        hit = jnp.where(places == here, jnp.ones((), BF16), jnp.zeros((), BF16))
        ref[row0 + part * 128 : row0 + (part + 1) * 128, lanes] = hit


def column_of(row):
    size = row.shape[1]
    same = lax.broadcasted_iota(I32, (size, size), 0) == lax.broadcasted_iota(I32, (size, size), 1)
    return jnp.sum(jnp.where(same, row, 0.0), axis=1, keepdims=True)


def normalise(values, gain):
    center = values - jnp.mean(values, axis=0, keepdims=True)
    spread = jnp.mean(center * center, axis=0, keepdims=True)
    return center * lax.rsqrt(spread + EPS) * gain


def kernel(
    nb,
    nt,
    *refs,
):
    sources, out_ref, held = refs[:INPUTS], refs[INPUTS], refs[INPUTS + 1 : 2 * INPUTS + 1]
    (
        signal,
        taps,
        conv_cat,
        inside,
        send_pick,
        local_pick,
        spread_pick,
        halo_send,
        halo_recv,
        pack,
        label_send,
        label_recv,
        live_rows,
        place,
        block_out,
        data_send,
        data_recv,
        serial_acc,
        key_rows,
        query_rows,
        value_rows,
        self_rows,
        heads_out,
        slot_acc,
        back_send,
        back_recv,
        halo_sems,
        label_sems,
        data_sems,
        back_sems,
        input_sems,
    ) = refs[2 * INPUTS + 1 :]
    loads = [pltpu.make_async_copy(sources[i], held[i], input_sems.at[i]) for i in range(INPUTS)]
    (
        feats,
        occupancy,
        adjacency,
        serial_pos,
        conv_one,
        conv_two,
        gain_one,
        gain_two,
        gain_attn,
        w_qkv,
        w_out,
        gain_mlp,
        w_up,
        w_down,
    ) = held
    channels, rows = feats.shape
    cap = pack.shape[0] // nt
    me_b = lax.axis_index("block")
    order = sorted(range(nt), key=lambda k: (-min(k, nt - k), k))
    me_t = lax.axis_index("token")

    barrier = pltpu.get_barrier_semaphore()
    for off in OFFS:
        pl.semaphore_signal(
            barrier, inc=1, device_id={"block": lax.rem(me_b + off + nb, nb)}, device_id_type=MESH
        )
    for load in loads:
        load.start()
    for k in range(1, nt):
        pl.semaphore_signal(
            barrier, inc=1, device_id={"token": lax.rem(me_t + k, nt)}, device_id_type=MESH
        )

    def halo_copy(step, o):
        return pltpu.make_async_remote_copy(
            src_ref=halo_send.at[step, o],
            dst_ref=halo_recv.at[step, o],
            send_sem=halo_sems.at[0, step, o],
            recv_sem=halo_sems.at[1, step, o],
            device_id={"block": lax.rem(me_b + OFFS[o] + nb, nb)},
            device_id_type=MESH,
        )

    def token_copy(source, target, sems, k, step):
        return pltpu.make_async_remote_copy(
            src_ref=source.at[k],
            dst_ref=target.at[k],
            send_sem=sems.at[0, k],
            recv_sem=sems.at[1, k],
            device_id={"token": lax.rem(me_t + step + nt, nt)},
            device_id_type=MESH,
        )

    label_copy = lambda k: token_copy(label_send, label_recv, label_sems, k, k)
    data_copy = lambda k: token_copy(data_send, data_recv, data_sems, k, k)


    def back_copy(wave, k):
        return pltpu.make_async_remote_copy(
            src_ref=back_send.at[k, WAVE_ROWS[wave]],
            dst_ref=back_recv.at[k, WAVE_ROWS[wave]],
            send_sem=back_sems.at[0, wave, k],
            recv_sem=back_sems.at[1, wave, k],
            device_id={"token": lax.rem(me_t - k + nt, nt)},
            device_id_type=MESH,
        )

    for i in range(4):
        loads[i].wait()
    owner = {}
    index = {}
    for f in range(6):
        for b in range(2):
            owner[f, b] = adjacency[0, b, f]
            index[f, b] = adjacency[1, b, f]
    pairs = [(f, b) for f in range(6) for b in range(2)]
    lane = lax.broadcasted_iota(I32, (1, 128), 1)
    half, within = lane >> 6, lane & 63
    voxel_of = [face_index(f, within) for f in range(6)]
    for o, off in enumerate(OFFS):
        target = me_b + off
        count = jnp.int32(0)
        voxel = jnp.full((1, 128), -1, I32)
        for f, b in pairs:
            match = (owner[f, b] >= 0) & (owner[f, b] == target)
            slot = jnp.where(match, count, -1)
            count = count + jnp.where(match, 1, 0)
            voxel = jnp.where(half == slot, voxel_of[f] + b * BLOCK, voxel)
        store_one_hot(send_pick, 0, rows, slice(o * 128, (o + 1) * 128), voxel)

    occupied = occupancy[...] > 0
    field = jnp.where(occupied, feats[...].astype(F32), 0.0)
    signal[...] = field.astype(BF16)

    def send_halo(step):
        payload = dot(signal[...] if step == 0 else taps[0:channels, :], send_pick[...]).astype(BF16)
        for o in range(4):
            halo_send[step, o] = payload[:, o * 128 : (o + 1) * 128]

    send_halo(0)

    pl.semaphore_wait(barrier, 4 + nt - 1)

    for o in range(4):
        halo_copy(0, o).start()

    takes = {}
    for a in range(3):
        for b in range(2):
            local_src = jnp.full((1, 128), -1, I32)
            source_of = []
            for side in range(2):
                f = 2 * a + side
                own, idx = owner[f, b], index[f, b]
                key = (f ^ 1) * 2 + idx
                slot = jnp.int32(0)
                for f2, b2 in pairs:
                    if (f2, b2) != (f, b):
                        before = (owner[f2, b2] == own) & ((f2 ^ 1) * 2 + index[f2, b2] < key)
                        slot = slot + jnp.where(before, 1, 0)
                gap = me_b - own
                from_o = jnp.where(gap < 0, gap + 2, gap + 1)
                source_of.append(jnp.where((own >= 0) & (gap != 0), from_o * 2 + slot, -1))
                base = jnp.where((own >= 0) & (gap == 0), idx * BLOCK, -4096)
                local_src = jnp.where(half == side, voxel_of[f ^ 1] + base, local_src)
            source = jnp.where(half == 0, source_of[0], source_of[1])
            for o in range(4):
                for cross in range(2):
                    hit = source == o * 2 + (half ^ cross)
                    takes[a, b, o, cross] = jnp.where(hit, 1.0, 0.0).astype(BF16)
            lanes = slice((a * 2 + b) * 128, (a * 2 + b + 1) * 128)
            store_one_hot(local_pick, 0, rows, lanes, local_src)
    side_row = lax.broadcasted_iota(I32, (128, BLOCK), 0)
    voxel_lane = lax.broadcasted_iota(I32, (128, BLOCK), 1)
    for a in (1, 2):
        lower = face_index(2 * a, side_row & 63)
        upper = face_index(2 * a + 1, side_row & 63)
        hit = voxel_lane == jnp.where(side_row < 64, lower, upper)
        spread_pick[a - 1] = jnp.where(hit, 1.0, 0.0).astype(BF16)

    spot = lax.broadcasted_iota(I32, (1, rows), 1) & (BLOCK - 1)
    edges = [spot < 64, spot >= 448, (spot >> 3) & 7 == 0, (spot >> 3) & 7 == 7, spot & 7 == 0, spot & 7 == 7]
    on_edge = [jnp.where(e, 1.0, 0.0) for e in edges]

    def convolve(step, source, weight):
        for t in range(7):
            conv_cat[:, t * channels : (t + 1) * channels] = weight[t]
        for f in range(6):
            moved = pltpu.roll(source, SHIFTS[f] % rows, 1) * (1.0 - on_edge[f])
            taps[(f + 1) * channels : (f + 2) * channels, :] = moved.astype(BF16)
        local = dot(taps[0:channels, :], local_pick[...]).astype(BF16)
        inside[...] = dot(conv_cat[...], taps[...])
        for o in range(4):
            halo_copy(step, o).wait_recv()
        came = [halo_recv[step, o] for o in range(4)]
        came = [(x, jnp.concatenate([x[:, FACE:], x[:, :FACE]], axis=1)) for x in came]

        def faces(a, b):
            piece = local[:, (a * 2 + b) * 128 : (a * 2 + b + 1) * 128]
            for o in range(4):
                for cross in range(2):
                    piece = piece + came[o][cross] * takes[a, b, o, cross]
            return piece

        tiles = [inside[:, c * 128 : (c + 1) * 128] for c in range(rows // 128)]
        per_block = BLOCK // 128
        for a in range(3):
            pair = weight[2 * a + 1 : 2 * a + 3].reshape(2 * channels, channels)
            sides = dot(pair, jnp.concatenate([faces(a, 0), faces(a, 1)], axis=1))
            edge = [
                jnp.where(half == 0, sides[:channels, lanes], sides[channels:, lanes])
                for lanes in (slice(0, 128), slice(128, 256))
            ]
            if a == 0:
                for b in range(2):
                    first, last = b * per_block, (b + 1) * per_block - 1
                    tiles[first] = tiles[first] + jnp.where(half == 0, edge[b], 0.0)
                    tiles[last] = tiles[last] + jnp.where(half == 1, edge[b], 0.0)
            else:
                high = [e.astype(BF16) for e in edge]
                low = [(e - h.astype(F32)).astype(BF16) for e, h in zip(edge, high)]
                wide = dot(jnp.concatenate(high + low, axis=0), spread_pick[a - 1])
                for b in range(2):
                    part = wide[b * channels : (b + 1) * channels] + wide[(b + 2) * channels : (b + 3) * channels]
                    for c in range(per_block):
                        t = b * per_block + c
                        tiles[t] = tiles[t] + part[:, c * 128 : (c + 1) * 128]
        return jnp.concatenate(tiles, axis=1)

    for i in range(4, INPUTS):
        loads[i].wait()
    taps[0:channels, :] = signal[...]
    summed = convolve(0, field, conv_one)
    middle = jnp.where(occupied, jnp.maximum(normalise(summed, column_of(gain_one[...])), 0.0), 0.0)
    middle = middle.astype(BF16)
    taps[0:channels, :] = middle
    send_halo(1)
    for o in range(4):
        halo_copy(1, o).start()

    position = serial_pos[...]
    relative = ((position >> 10) - me_t + nt) & (nt - 1)
    sub16 = lax.broadcasted_iota(I32, (16, rows), 0)
    member = jnp.where(sub16 == relative, 1.0, 0.0)
    upto = lax.broadcasted_iota(I32, (128, 128), 0) <= lax.broadcasted_iota(I32, (128, 128), 1)
    upto = jnp.where(upto, 1.0, 0.0).astype(BF16)
    chunks = rows // 128
    stacked = jnp.concatenate(
        [member[:, c * 128 : (c + 1) * 128] for c in range(chunks)], axis=0
    ).astype(BF16)
    prefix = dot(stacked, upto)
    carry = jnp.zeros((16, 1), F32)
    ranks = []
    for c in range(chunks):
        piece = prefix[c * 16 : (c + 1) * 16, :]
        ranks.append(piece + carry - 1.0)
        carry = carry + piece[:, 127:128]
    slots = jnp.where(member > 0.5, jnp.concatenate(ranks, axis=1), -1.0).astype(I32)
    for k in range(nt):
        store_one_hot(pack, k * cap, cap, slice(0, rows), slots[k : k + 1, :])
    target_row = position & (rows - 1)
    facts = jnp.where(
        sub16 == 0,
        target_row >> 5,
        jnp.where(
            sub16 == 1,
            target_row & 31,
            jnp.where(sub16 == 2, jnp.where(occupied, 1, 0), jnp.where(sub16 == 3, 1, 0)),
        ),
    )
    facts = dot_nt(facts.astype(F32).astype(BF16), pack[...])
    goes_to = jnp.where(facts[3:4, :] > 0.5, facts[0:1, :] * 32.0 + facts[1:2, :], -1.0)
    sub8 = lax.broadcasted_iota(I32, (8, goes_to.shape[1]), 0)
    labels = jnp.where(sub8 == 0, goes_to, jnp.where(sub8 == 1, facts[2:3, :], 0.0))
    for k in range(nt):
        part = labels[:, k * cap : (k + 1) * cap]
        if k == 0:
            label_recv[0] = part
        else:
            label_send[k] = part

    for k in range(1, nt):
        label_copy(k).start()

    summed = convolve(1, middle.astype(F32), conv_two)
    result = jnp.maximum(signal[...].astype(F32) + normalise(summed, column_of(gain_two[...])), 0.0)
    result = jnp.where(occupied, result, 0.0).astype(BF16)
    block_out[...] = result
    normed = normalise(result.astype(F32), column_of(gain_attn[...])).astype(BF16)

    for ks in [order[:2], order[2:4]] + [order[g : g + GROUP] for g in range(4, nt, GROUP)]:
        chosen = jnp.concatenate([pack[k * cap : (k + 1) * cap, :] for k in ks], axis=0)
        packed = dot_nt(normed, chosen).astype(BF16)
        for j, k in enumerate(ks):
            part = packed[:, j * cap : (j + 1) * cap]
            if k == 0:
                data_recv[0] = part
            else:
                data_send[k] = part
                data_copy(k).start()

    for k in range(1, nt):
        label_copy(k).wait_recv()
    for k in range(nt):
        label = label_recv[k]
        lanes = slice(k * cap, (k + 1) * cap)
        store_one_hot(place, 0, rows, lanes, label[0:1, :].astype(I32))
        live_rows[:, lanes] = jnp.broadcast_to(label[1:2, :], (16, cap)).astype(BF16)
    query_rows[...] = jnp.zeros_like(query_rows)
    w_out_here = w_out[...].astype(F32).T.astype(BF16)
    w_up_here = w_up[...].astype(F32).T.astype(BF16)
    arrivals = [order[: nt // 2], order[nt // 2 : 3 * nt // 4], order[3 * nt // 4 :]]
    for g, ks in enumerate(arrivals):
        for k in ks:
            if k:
                data_copy(k).wait_recv()
        came = jnp.concatenate(
            [
                jnp.concatenate([data_recv[k], live_rows[:, k * cap : (k + 1) * cap]], axis=0)
                for k in ks
            ],
            axis=1,
        )
        chosen = jnp.concatenate([place[:, k * cap : (k + 1) * cap] for k in ks], axis=1)
        part = dot_nt(came, chosen)
        serial_acc[...] = part if g == 0 else serial_acc[...] + part

    groups = [order[g * GROUP : (g + 1) * GROUP] for g in range(nt // GROUP)]
    live = serial_acc[channels : channels + 1, :] > 0.5
    width = HEADS * HD
    projected = dot(w_qkv[...], serial_acc[0:channels, :].astype(BF16))
    scaled = projected[:width, :] * (math.log2(math.e) / math.sqrt(HD))
    query_high = scaled.astype(BF16).astype(F32)
    query_low = scaled - query_high
    keys = projected[width : 2 * width, :]
    key_high = keys.astype(BF16).astype(F32)
    key_low = keys - key_high
    values = projected[2 * width :, :]
    sub8 = lax.broadcasted_iota(I32, (8, rows), 0)
    ones8 = jnp.where(sub8 == 0, 1.0, 0.0)
    bias8 = jnp.where((sub8 == 0) & jnp.logical_not(live), AWAY, 0.0)
    key_parts = []
    patches = rows // PATCH
    for h in range(HEADS):
        own = slice(h * HD, (h + 1) * HD)
        key_parts += [key_high[own], key_low[own], key_high[own], bias8]
        query = jnp.concatenate([query_high[own], query_high[own], query_low[own], ones8], axis=0).astype(BF16)
        value_rows[h * 16 : (h + 1) * 16, :] = jnp.concatenate([values[own], ones8], axis=0).astype(BF16)
        for p in range(patches):
            query_rows[p * HEADS + h, h % SET * 32 : (h % SET + 1) * 32, :] = query[:, p * PATCH : (p + 1) * PATCH]
        alone = jnp.sum(scaled[own] * keys[own], axis=0, keepdims=True)
        self_rows[h] = jnp.where(live, AWAY, alone)
    key_rows[...] = jnp.concatenate(key_parts, axis=0).astype(BF16).T

    def score(p, h, q):
        first = h // SET * SET
        last = min(first + SET, HEADS)
        return dot(
            key_rows[p * PATCH : (p + 1) * PATCH, first * 32 : last * 32],
            query_rows[p * HEADS + h, 0 : (last - first) * 32, q * QCOLS : (q + 1) * QCOLS],
        )

    def attend(p, h, q, scores):
        keys_of = slice(p * PATCH, (p + 1) * PATCH)
        cols = slice(p * PATCH + q * QCOLS, p * PATCH + (q + 1) * QCOLS)
        alone = self_rows[h, :, cols]
        largest = jnp.maximum(jnp.max(scores, axis=0, keepdims=True), alone)
        weights = jnp.exp2(scores - largest).astype(BF16)
        sums = dot(value_rows[h * 16 : (h + 1) * 16, keys_of], weights)
        value = value_rows[h * 16 : (h + 1) * 16, cols]
        own = jnp.exp2(alone - largest)
        top = sums[0:HD] + own * value[0:HD].astype(F32)
        heads_out[h * HD : (h + 1) * HD, cols] = top / (sums[HD : HD + 1] + own)

    def to_slots(wave, p, ks):
        heads = WAVES[wave]
        part = heads_out[heads[0] * HD : (heads[-1] + 1) * HD, p * PATCH : (p + 1) * PATCH].astype(BF16)
        chosen = [place[p * PATCH : (p + 1) * PATCH, k * cap : (k + 1) * cap] for k in ks]
        return dot(part, jnp.concatenate(chosen, axis=1))

    def add_slots(wave, p):
        for g, ks in enumerate(groups):
            part = to_slots(wave, p, ks)
            slot_acc[g, WAVE_ROWS[wave]] = part if p == 0 else slot_acc[g, WAVE_ROWS[wave]] + part

    def give_back(wave, last):
        for g, ks in enumerate(groups):
            back = slot_acc[g, WAVE_ROWS[wave]]
            if last:
                back = back + to_slots(wave, patches - 1, ks)
            back = back.astype(BF16)
            for j, k in enumerate(ks):
                part = back[:, j * cap : (j + 1) * cap]
                if k == 0:
                    back_recv[0, WAVE_ROWS[wave]] = part
                else:
                    back_send[k, WAVE_ROWS[wave]] = part
                    if last:
                        back_copy(wave, k).start()
        if not last:
            for k in order:
                if k:
                    back_copy(wave, k).start()

    units = [(wave, p, h, q) for wave in range(2) for p in range(patches) for h in WAVES[wave] for q in range(PATCH // QCOLS)]
    ahead = [score(*unit[1:]) for unit in units[:4]]
    waiting = []
    for i, (wave, p, h, q) in enumerate(units):
        scores = ahead.pop(0)
        if i + 4 < len(units):
            ahead.append(score(*units[i + 4][1:]))
        attend(p, h, q, scores)
        if waiting and h == WAVES[wave][0] and q == 0:
            done = waiting.pop()
            add_slots(*done)
            if done == (0, patches - 1):
                give_back(0, False)
        if h == WAVES[wave][-1] and q == PATCH // QCOLS - 1:
            waiting.append((wave, p))
    give_back(1, True)

    returned = None
    nearest = order[::-1]
    for g, ks in enumerate([nearest[: nt // 2], nearest[nt // 2 : 3 * nt // 4], nearest[3 * nt // 4 :]]):
        for k in ks:
            if k:
                for wave in range(2):
                    back_copy(wave, k).wait_recv()
        came = jnp.concatenate([back_recv[k] for k in ks], axis=1)
        part = dot(came, jnp.concatenate([pack[k * cap : (k + 1) * cap, :] for k in ks], axis=0))
        returned = part if g == 0 else returned + part
    attended = dot(w_out_here, returned.astype(BF16)).astype(BF16)
    gain = column_of(gain_mlp[...])
    for c in range(0, rows, 256):
        cols = slice(c, c + 256)
        combined = block_out[:, cols].astype(F32) + attended[:, cols].astype(F32)
        hidden = dot(w_up_here, normalise(combined, gain).astype(BF16))
        inner = hidden * (GELU_ONE + GELU_THREE * (hidden * hidden))
        hidden = (hidden + hidden * jnp.tanh(inner)).astype(BF16)
        summed = combined + 0.5 * dot(w_down[...], hidden)
        out_ref[:, cols] = jnp.where(occupied[:, cols], summed, 0.0).astype(BF16)

    for step in range(2):
        for o in range(4):
            halo_copy(step, o).wait_send()
    for k in range(1, nt):
        label_copy(k).wait_send()
        data_copy(k).wait_send()
        for wave in range(2):
            back_copy(wave, k).wait_send()


def per_device(nb, nt, feats, occupancy, adjacency, serial_pos, conv_one, conv_two, gain_one, gain_two, gain_attn, w_qkv, w_out, gain_mlp, w_up, w_down):
    channels, rows = feats.shape
    slots = 2 * rows
    cap = slots // nt
    width = HEADS * HD
    row = lambda x: x.reshape(1, -1)
    patches = rows // PATCH
    inputs = (
        feats,
        row(occupancy),
        adjacency.transpose(0, 2, 1),
        row(serial_pos),
        conv_one,
        conv_two,
        row(gain_one),
        row(gain_two),
        row(gain_attn),
        w_qkv,
        w_out.T,
        row(gain_mlp),
        w_up.T,
        w_down,
    )
    return pl.pallas_call(
        functools.partial(kernel, nb, nt),
        out_shape=jax.ShapeDtypeStruct((channels, rows), BF16),
        in_specs=[pl.BlockSpec(memory_space=pltpu.HBM)] * INPUTS,
        out_specs=pl.BlockSpec(memory_space=pltpu.VMEM),
        scratch_shapes=[
            pltpu.SMEM(x.shape, x.dtype) if i == 2 else pltpu.VMEM(x.shape, x.dtype)
            for i, x in enumerate(inputs)
        ]
        + [
            pltpu.VMEM((channels, rows), BF16),
            pltpu.VMEM((7 * channels, rows), BF16),
            pltpu.VMEM((channels, 7 * channels), BF16),
            pltpu.VMEM((channels, rows), F32),
            pltpu.VMEM((rows, 512), BF16),
            pltpu.VMEM((rows, 768), BF16),
            pltpu.VMEM((2, 128, BLOCK), BF16),
            pltpu.VMEM((2, 4, channels, 128), BF16),
            pltpu.VMEM((2, 4, channels, 128), BF16),
            pltpu.VMEM((slots, rows), BF16),
            pltpu.VMEM((nt, 8, cap), F32),
            pltpu.VMEM((nt, 8, cap), F32),
            pltpu.VMEM((16, slots), BF16),
            pltpu.VMEM((rows, slots), BF16),
            pltpu.VMEM((channels, rows), BF16),
            pltpu.VMEM((nt, channels, cap), BF16),
            pltpu.VMEM((nt, channels, cap), BF16),
            pltpu.VMEM((channels + 16, rows), F32),
            pltpu.VMEM((rows, HEADS * 32), BF16),
            pltpu.VMEM((patches * HEADS, SET * 32, PATCH), BF16),
            pltpu.VMEM((HEADS * 16, rows), BF16),
            pltpu.VMEM((HEADS, 1, rows), F32),
            pltpu.VMEM((width, rows), F32),
            pltpu.VMEM((nt // GROUP, width, GROUP * cap), F32),
            pltpu.VMEM((nt, width, cap), BF16),
            pltpu.VMEM((nt, width, cap), BF16),
            pltpu.SemaphoreType.DMA((2, 2, 4)),
            pltpu.SemaphoreType.DMA((2, nt)),
            pltpu.SemaphoreType.DMA((2, nt)),
            pltpu.SemaphoreType.DMA((2, 2, nt)),
            pltpu.SemaphoreType.DMA((INPUTS,)),
        ],
        compiler_params=pltpu.CompilerParams(
            collective_id=0, has_side_effects=True, vmem_limit_bytes=VMEM_LIMIT
        ),
        name="voxel_step",
    )(*[pltpu.with_memory_space_constraint(x, pltpu.HBM) for x in inputs])


def solution(mesh):
    nb, nt = mesh.shape["block"], mesh.shape["token"]
    split = ("block", "token")
    in_specs = (P(None, split), P(split), P(None, None, split), P(split)) + (P(),) * 10
    return jax.shard_map(
        functools.partial(per_device, nb, nt),
        mesh=mesh,
        in_specs=in_specs,
        out_specs=P(None, split),
        check_vma=False,
    )
```

```python
import functools
import math

import jax
import jax.numpy as jnp
from jax import lax
from jax.experimental import pallas as pl
from jax.experimental.pallas import tpu as pltpu
from jax.sharding import PartitionSpec as P

MESH = pl.DeviceIdType.MESH
F32 = jnp.float32
BF16 = jnp.bfloat16
I32 = jnp.int32

HEADS = 6
HD = 8
PATCH = 512
BLOCK = 512
FACE = 64
EPS = 1e-05
OFFS = (-2, -1, 1, 2)
SHIFTS = (64, -64, 8, -8, 1, -1)
AWAY = -1e30
NT_DIMS = (((1,), (1,)), ((), ()))
SET = 4
QCOLS = 256
GROUP = 4
INPUTS = 14
WAVES = ((0, 1, 2, 3), (4, 5))
WAVE_ROWS = (slice(0, 32), slice(32, 48))
GELU_ONE = math.sqrt(2 / math.pi)
GELU_THREE = GELU_ONE * 0.044715
VMEM_LIMIT = 36 * 1024 * 1024


def dot(a, b):
    return jnp.dot(a, b, preferred_element_type=F32)


def dot_nt(a, b):
    return lax.dot_general(a, b, NT_DIMS, preferred_element_type=F32)


def face_index(face, place):
    high, low = place >> 3, place & 7
    if face == 0:
        return place
    if face == 1:
        return place + 448
    if face == 2:
        return high * 64 + low
    if face == 3:
        return high * 64 + low + 56
    if face == 4:
        return place * 8
    return place * 8 + 7


def store_one_hot(ref, row0, rows, lanes, index):
    width = index.shape[1]
    places = lax.broadcasted_iota(I32, (128, width), 0).astype(F32).astype(BF16)
    for part in range(rows // 128):
        here = jnp.where(index >> 7 == part, index & 127, -1).astype(F32).astype(BF16)
        hit = jnp.where(places == here, jnp.ones((), BF16), jnp.zeros((), BF16))
        ref[row0 + part * 128 : row0 + (part + 1) * 128, lanes] = hit


def column_of(row):
    size = row.shape[1]
    same = lax.broadcasted_iota(I32, (size, size), 0) == lax.broadcasted_iota(I32, (size, size), 1)
    return jnp.sum(jnp.where(same, row, 0.0), axis=1, keepdims=True)


def normalise(values, gain):
    center = values - jnp.mean(values, axis=0, keepdims=True)
    spread = jnp.mean(center * center, axis=0, keepdims=True)
    return center * lax.rsqrt(spread + EPS) * gain


def kernel(
    nb,
    nt,
    *refs,
):
    sources, out_ref, held = refs[:INPUTS], refs[INPUTS], refs[INPUTS + 1 : 2 * INPUTS + 1]
    (
        signal,
        taps,
        conv_cat,
        inside,
        send_pick,
        local_pick,
        spread_pick,
        halo_send,
        halo_recv,
        pack,
        label_send,
        label_recv,
        live_rows,
        place,
        block_out,
        data_send,
        data_recv,
        serial_acc,
        key_rows,
        query_rows,
        value_rows,
        self_rows,
        heads_out,
        slot_acc,
        back_send,
        back_recv,
        halo_sems,
        label_sems,
        data_sems,
        back_sems,
        input_sems,
    ) = refs[2 * INPUTS + 1 :]
    loads = [pltpu.make_async_copy(sources[i], held[i], input_sems.at[i]) for i in range(INPUTS)]
    (
        feats,
        occupancy,
        adjacency,
        serial_pos,
        conv_one,
        conv_two,
        gain_one,
        gain_two,
        gain_attn,
        w_qkv,
        w_out,
        gain_mlp,
        w_up,
        w_down,
    ) = held
    channels, rows = feats.shape
    cap = pack.shape[0] // nt
    me_b = lax.axis_index("block")
    order = sorted(range(nt), key=lambda k: (-min(k, nt - k), k))
    me_t = lax.axis_index("token")

    barrier = pltpu.get_barrier_semaphore()
    for off in OFFS:
        pl.semaphore_signal(
            barrier, inc=1, device_id={"block": lax.rem(me_b + off + nb, nb)}, device_id_type=MESH
        )
    for load in loads:
        load.start()
    for k in order[:-1]:
        pl.semaphore_signal(
            barrier, inc=1, device_id={"token": lax.rem(me_t + k, nt)}, device_id_type=MESH
        )

    def halo_copy(step, o):
        return pltpu.make_async_remote_copy(
            src_ref=halo_send.at[step, o],
            dst_ref=halo_recv.at[step, o],
            send_sem=halo_sems.at[0, step, o],
            recv_sem=halo_sems.at[1, step, o],
            device_id={"block": lax.rem(me_b + OFFS[o] + nb, nb)},
            device_id_type=MESH,
        )

    def token_copy(source, target, sems, k, step):
        return pltpu.make_async_remote_copy(
            src_ref=source.at[k],
            dst_ref=target.at[k],
            send_sem=sems.at[0, k],
            recv_sem=sems.at[1, k],
            device_id={"token": lax.rem(me_t + step + nt, nt)},
            device_id_type=MESH,
        )

    label_copy = lambda k: token_copy(label_send, label_recv, label_sems, k, k)
    data_copy = lambda k: token_copy(data_send, data_recv, data_sems, k, k)


    def back_copy(wave, k):
        return pltpu.make_async_remote_copy(
            src_ref=back_send.at[k, WAVE_ROWS[wave]],
            dst_ref=back_recv.at[k, WAVE_ROWS[wave]],
            send_sem=back_sems.at[0, wave, k],
            recv_sem=back_sems.at[1, wave, k],
            device_id={"token": lax.rem(me_t - k + nt, nt)},
            device_id_type=MESH,
        )

    for i in range(4):
        loads[i].wait()
    owner = {}
    index = {}
    for f in range(6):
        for b in range(2):
            owner[f, b] = adjacency[0, b, f]
            index[f, b] = adjacency[1, b, f]
    pairs = [(f, b) for f in range(6) for b in range(2)]
    lane = lax.broadcasted_iota(I32, (1, 128), 1)
    half, within = lane >> 6, lane & 63
    voxel_of = [face_index(f, within) for f in range(6)]
    for o, off in enumerate(OFFS):
        target = me_b + off
        count = jnp.int32(0)
        voxel = jnp.full((1, 128), -1, I32)
        for f, b in pairs:
            match = (owner[f, b] >= 0) & (owner[f, b] == target)
            slot = jnp.where(match, count, -1)
            count = count + jnp.where(match, 1, 0)
            voxel = jnp.where(half == slot, voxel_of[f] + b * BLOCK, voxel)
        store_one_hot(send_pick, 0, rows, slice(o * 128, (o + 1) * 128), voxel)

    occupied = occupancy[...] > 0
    field = jnp.where(occupied, feats[...].astype(F32), 0.0)
    signal[...] = field.astype(BF16)

    def send_halo(step):
        payload = dot(signal[...] if step == 0 else taps[0:channels, :], send_pick[...]).astype(BF16)
        for o in range(4):
            halo_send[step, o] = payload[:, o * 128 : (o + 1) * 128]

    send_halo(0)

    pl.semaphore_wait(barrier, 4 + nt - 1)

    for o in range(4):
        halo_copy(0, o).start()

    takes = {}
    for a in range(3):
        for b in range(2):
            local_src = jnp.full((1, 128), -1, I32)
            source_of = []
            for side in range(2):
                f = 2 * a + side
                own, idx = owner[f, b], index[f, b]
                key = (f ^ 1) * 2 + idx
                slot = jnp.int32(0)
                for f2, b2 in pairs:
                    if (f2, b2) != (f, b):
                        before = (owner[f2, b2] == own) & ((f2 ^ 1) * 2 + index[f2, b2] < key)
                        slot = slot + jnp.where(before, 1, 0)
                gap = me_b - own
                from_o = jnp.where(gap < 0, gap + 2, gap + 1)
                source_of.append(jnp.where((own >= 0) & (gap != 0), from_o * 2 + slot, -1))
                base = jnp.where((own >= 0) & (gap == 0), idx * BLOCK, -4096)
                local_src = jnp.where(half == side, voxel_of[f ^ 1] + base, local_src)
            source = jnp.where(half == 0, source_of[0], source_of[1])
            for o in range(4):
                for cross in range(2):
                    hit = source == o * 2 + (half ^ cross)
                    takes[a, b, o, cross] = jnp.where(hit, 1.0, 0.0).astype(BF16)
            lanes = slice((a * 2 + b) * 128, (a * 2 + b + 1) * 128)
            store_one_hot(local_pick, 0, rows, lanes, local_src)
    side_row = lax.broadcasted_iota(I32, (128, BLOCK), 0)
    voxel_lane = lax.broadcasted_iota(I32, (128, BLOCK), 1)
    for a in (1, 2):
        lower = face_index(2 * a, side_row & 63)
        upper = face_index(2 * a + 1, side_row & 63)
        hit = voxel_lane == jnp.where(side_row < 64, lower, upper)
        spread_pick[a - 1] = jnp.where(hit, 1.0, 0.0).astype(BF16)

    spot = lax.broadcasted_iota(I32, (1, rows), 1) & (BLOCK - 1)
    edges = [spot < 64, spot >= 448, (spot >> 3) & 7 == 0, (spot >> 3) & 7 == 7, spot & 7 == 0, spot & 7 == 7]
    on_edge = [jnp.where(e, 1.0, 0.0) for e in edges]

    def convolve(step, source, weight):
        for t in range(7):
            conv_cat[:, t * channels : (t + 1) * channels] = weight[t]
        for f in range(6):
            moved = pltpu.roll(source, SHIFTS[f] % rows, 1) * (1.0 - on_edge[f])
            taps[(f + 1) * channels : (f + 2) * channels, :] = moved.astype(BF16)
        local = dot(taps[0:channels, :], local_pick[...]).astype(BF16)
        inside[...] = dot(conv_cat[...], taps[...])
        for o in range(4):
            halo_copy(step, o).wait_recv()
        came = [halo_recv[step, o] for o in range(4)]
        came = [(x, jnp.concatenate([x[:, FACE:], x[:, :FACE]], axis=1)) for x in came]

        def faces(a, b):
            piece = local[:, (a * 2 + b) * 128 : (a * 2 + b + 1) * 128]
            for o in range(4):
                for cross in range(2):
                    piece = piece + came[o][cross] * takes[a, b, o, cross]
            return piece

        tiles = [inside[:, c * 128 : (c + 1) * 128] for c in range(rows // 128)]
        per_block = BLOCK // 128
        for a in range(3):
            pair = weight[2 * a + 1 : 2 * a + 3].reshape(2 * channels, channels)
            sides = dot(pair, jnp.concatenate([faces(a, 0), faces(a, 1)], axis=1))
            edge = [
                jnp.where(half == 0, sides[:channels, lanes], sides[channels:, lanes])
                for lanes in (slice(0, 128), slice(128, 256))
            ]
            if a == 0:
                for b in range(2):
                    first, last = b * per_block, (b + 1) * per_block - 1
                    tiles[first] = tiles[first] + jnp.where(half == 0, edge[b], 0.0)
                    tiles[last] = tiles[last] + jnp.where(half == 1, edge[b], 0.0)
            else:
                high = [e.astype(BF16) for e in edge]
                low = [(e - h.astype(F32)).astype(BF16) for e, h in zip(edge, high)]
                wide = dot(jnp.concatenate(high + low, axis=0), spread_pick[a - 1])
                for b in range(2):
                    part = wide[b * channels : (b + 1) * channels] + wide[(b + 2) * channels : (b + 3) * channels]
                    for c in range(per_block):
                        t = b * per_block + c
                        tiles[t] = tiles[t] + part[:, c * 128 : (c + 1) * 128]
        return jnp.concatenate(tiles, axis=1)

    for i in range(4, INPUTS):
        loads[i].wait()
    taps[0:channels, :] = signal[...]
    summed = convolve(0, field, conv_one)
    middle = jnp.where(occupied, jnp.maximum(normalise(summed, column_of(gain_one[...])), 0.0), 0.0)
    middle = middle.astype(BF16)
    taps[0:channels, :] = middle
    send_halo(1)
    for o in range(4):
        halo_copy(1, o).start()

    position = serial_pos[...]
    relative = ((position >> 10) - me_t + nt) & (nt - 1)
    sub16 = lax.broadcasted_iota(I32, (16, rows), 0)
    member = jnp.where(sub16 == relative, 1.0, 0.0)
    upto = lax.broadcasted_iota(I32, (128, 128), 0) <= lax.broadcasted_iota(I32, (128, 128), 1)
    upto = jnp.where(upto, 1.0, 0.0).astype(BF16)
    chunks = rows // 128
    stacked = jnp.concatenate(
        [member[:, c * 128 : (c + 1) * 128] for c in range(chunks)], axis=0
    ).astype(BF16)
    prefix = dot(stacked, upto)
    carry = jnp.zeros((16, 1), F32)
    ranks = []
    for c in range(chunks):
        piece = prefix[c * 16 : (c + 1) * 16, :]
        ranks.append(piece + carry - 1.0)
        carry = carry + piece[:, 127:128]
    slots = jnp.where(member > 0.5, jnp.concatenate(ranks, axis=1), -1.0).astype(I32)
    for k in range(nt):
        store_one_hot(pack, k * cap, cap, slice(0, rows), slots[k : k + 1, :])
    target_row = position & (rows - 1)
    facts = jnp.where(
        sub16 == 0,
        target_row >> 5,
        jnp.where(
            sub16 == 1,
            target_row & 31,
            jnp.where(sub16 == 2, jnp.where(occupied, 1, 0), jnp.where(sub16 == 3, 1, 0)),
        ),
    )
    facts = dot_nt(facts.astype(F32).astype(BF16), pack[...])
    goes_to = jnp.where(facts[3:4, :] > 0.5, facts[0:1, :] * 32.0 + facts[1:2, :], -1.0)
    sub8 = lax.broadcasted_iota(I32, (8, goes_to.shape[1]), 0)
    labels = jnp.where(sub8 == 0, goes_to, jnp.where(sub8 == 1, facts[2:3, :], 0.0))
    for k in range(nt):
        part = labels[:, k * cap : (k + 1) * cap]
        if k == 0:
            label_recv[0] = part
        else:
            label_send[k] = part

    for k in range(1, nt):
        label_copy(k).start()

    summed = convolve(1, middle.astype(F32), conv_two)
    result = jnp.maximum(signal[...].astype(F32) + normalise(summed, column_of(gain_two[...])), 0.0)
    result = jnp.where(occupied, result, 0.0).astype(BF16)
    block_out[...] = result
    normed = normalise(result.astype(F32), column_of(gain_attn[...])).astype(BF16)

    for ks in [order[:2], order[2:4]] + [order[g : g + GROUP] for g in range(4, nt, GROUP)]:
        chosen = jnp.concatenate([pack[k * cap : (k + 1) * cap, :] for k in ks], axis=0)
        packed = dot_nt(normed, chosen).astype(BF16)
        for j, k in enumerate(ks):
            part = packed[:, j * cap : (j + 1) * cap]
            if k == 0:
                data_recv[0] = part
            else:
                data_send[k] = part
                data_copy(k).start()

    for k in range(1, nt):
        label_copy(k).wait_recv()
    for k in range(nt):
        label = label_recv[k]
        lanes = slice(k * cap, (k + 1) * cap)
        store_one_hot(place, 0, rows, lanes, label[0:1, :].astype(I32))
        live_rows[:, lanes] = jnp.broadcast_to(label[1:2, :], (16, cap)).astype(BF16)
    query_rows[...] = jnp.zeros_like(query_rows)
    w_out_here = w_out[...].astype(F32).T.astype(BF16)
    w_up_here = w_up[...].astype(F32).T.astype(BF16)
    arrivals = [order[: nt // 2], order[nt // 2 : 3 * nt // 4], order[3 * nt // 4 :]]
    for g, ks in enumerate(arrivals):
        for k in ks:
            if k:
                data_copy(k).wait_recv()
        came = jnp.concatenate(
            [
                jnp.concatenate([data_recv[k], live_rows[:, k * cap : (k + 1) * cap]], axis=0)
                for k in ks
            ],
            axis=1,
        )
        chosen = jnp.concatenate([place[:, k * cap : (k + 1) * cap] for k in ks], axis=1)
        part = dot_nt(came, chosen)
        serial_acc[...] = part if g == 0 else serial_acc[...] + part

    groups = [order[g * GROUP : (g + 1) * GROUP] for g in range(nt // GROUP)]
    live = serial_acc[channels : channels + 1, :] > 0.5
    width = HEADS * HD
    projected = dot(w_qkv[...], serial_acc[0:channels, :].astype(BF16))
    scaled = projected[:width, :] * (math.log2(math.e) / math.sqrt(HD))
    query_high = scaled.astype(BF16).astype(F32)
    query_low = scaled - query_high
    keys = projected[width : 2 * width, :]
    key_high = keys.astype(BF16).astype(F32)
    key_low = keys - key_high
    values = projected[2 * width :, :]
    sub8 = lax.broadcasted_iota(I32, (8, rows), 0)
    ones8 = jnp.where(sub8 == 0, 1.0, 0.0)
    bias8 = jnp.where((sub8 == 0) & jnp.logical_not(live), AWAY, 0.0)
    key_parts = []
    patches = rows // PATCH
    for h in range(HEADS):
        own = slice(h * HD, (h + 1) * HD)
        key_parts += [key_high[own], key_low[own], key_high[own], bias8]
        query = jnp.concatenate([query_high[own], query_high[own], query_low[own], ones8], axis=0).astype(BF16)
        value_rows[h * 16 : (h + 1) * 16, :] = jnp.concatenate([values[own], ones8], axis=0).astype(BF16)
        for p in range(patches):
            query_rows[p * HEADS + h, h % SET * 32 : (h % SET + 1) * 32, :] = query[:, p * PATCH : (p + 1) * PATCH]
        alone = jnp.sum(scaled[own] * keys[own], axis=0, keepdims=True)
        self_rows[h] = jnp.where(live, AWAY, alone)
    key_rows[...] = jnp.concatenate(key_parts, axis=0).astype(BF16).T

    def score(p, h, q):
        first = h // SET * SET
        last = min(first + SET, HEADS)
        return dot(
            key_rows[p * PATCH : (p + 1) * PATCH, first * 32 : last * 32],
            query_rows[p * HEADS + h, 0 : (last - first) * 32, q * QCOLS : (q + 1) * QCOLS],
        )

    def attend(p, h, q, scores):
        keys_of = slice(p * PATCH, (p + 1) * PATCH)
        cols = slice(p * PATCH + q * QCOLS, p * PATCH + (q + 1) * QCOLS)
        alone = self_rows[h, :, cols]
        largest = jnp.maximum(jnp.max(scores, axis=0, keepdims=True), alone)
        weights = jnp.exp2(scores - largest).astype(BF16)
        sums = dot(value_rows[h * 16 : (h + 1) * 16, keys_of], weights)
        value = value_rows[h * 16 : (h + 1) * 16, cols]
        own = jnp.exp2(alone - largest)
        top = sums[0:HD] + own * value[0:HD].astype(F32)
        heads_out[h * HD : (h + 1) * HD, cols] = top / (sums[HD : HD + 1] + own)

    def to_slots(wave, p, ks):
        heads = WAVES[wave]
        part = heads_out[heads[0] * HD : (heads[-1] + 1) * HD, p * PATCH : (p + 1) * PATCH].astype(BF16)
        chosen = [place[p * PATCH : (p + 1) * PATCH, k * cap : (k + 1) * cap] for k in ks]
        return dot(part, jnp.concatenate(chosen, axis=1))

    def add_slots(wave, p):
        for g, ks in enumerate(groups):
            part = to_slots(wave, p, ks)
            slot_acc[g, WAVE_ROWS[wave]] = part if p == 0 else slot_acc[g, WAVE_ROWS[wave]] + part

    def give_back(wave, last):
        for g, ks in enumerate(groups):
            back = slot_acc[g, WAVE_ROWS[wave]]
            if last:
                back = back + to_slots(wave, patches - 1, ks)
            back = back.astype(BF16)
            for j, k in enumerate(ks):
                part = back[:, j * cap : (j + 1) * cap]
                if k == 0:
                    back_recv[0, WAVE_ROWS[wave]] = part
                else:
                    back_send[k, WAVE_ROWS[wave]] = part
                    if last:
                        back_copy(wave, k).start()
        if not last:
            for k in order:
                if k:
                    back_copy(wave, k).start()

    units = [(wave, p, h, q) for wave in range(2) for p in range(patches) for h in WAVES[wave] for q in range(PATCH // QCOLS)]
    ahead = [score(*unit[1:]) for unit in units[:4]]
    waiting = []
    for i, (wave, p, h, q) in enumerate(units):
        scores = ahead.pop(0)
        if i + 4 < len(units):
            ahead.append(score(*units[i + 4][1:]))
        attend(p, h, q, scores)
        if waiting and h == WAVES[wave][0] and q == 0:
            done = waiting.pop()
            add_slots(*done)
            if done == (0, patches - 1):
                give_back(0, False)
        if h == WAVES[wave][-1] and q == PATCH // QCOLS - 1:
            waiting.append((wave, p))
    give_back(1, True)

    returned = None
    nearest = order[::-1]
    for g, ks in enumerate([nearest[: nt // 2], nearest[nt // 2 : 3 * nt // 4], nearest[3 * nt // 4 :]]):
        for k in ks:
            if k:
                for wave in range(2):
                    back_copy(wave, k).wait_recv()
        came = jnp.concatenate([back_recv[k] for k in ks], axis=1)
        part = dot(came, jnp.concatenate([pack[k * cap : (k + 1) * cap, :] for k in ks], axis=0))
        returned = part if g == 0 else returned + part
    attended = dot(w_out_here, returned.astype(BF16)).astype(BF16)
    gain = column_of(gain_mlp[...])
    for c in range(0, rows, 256):
        cols = slice(c, c + 256)
        combined = block_out[:, cols].astype(F32) + attended[:, cols].astype(F32)
        hidden = dot(w_up_here, normalise(combined, gain).astype(BF16))
        inner = hidden * (GELU_ONE + GELU_THREE * (hidden * hidden))
        hidden = (hidden + hidden * jnp.tanh(inner)).astype(BF16)
        summed = combined + 0.5 * dot(w_down[...], hidden)
        out_ref[:, cols] = jnp.where(occupied[:, cols], summed, 0.0).astype(BF16)

    for step in range(2):
        for o in range(4):
            halo_copy(step, o).wait_send()
    for k in range(1, nt):
        label_copy(k).wait_send()
        data_copy(k).wait_send()
        for wave in range(2):
            back_copy(wave, k).wait_send()


def per_device(nb, nt, feats, occupancy, adjacency, serial_pos, conv_one, conv_two, gain_one, gain_two, gain_attn, w_qkv, w_out, gain_mlp, w_up, w_down):
    channels, rows = feats.shape
    slots = 2 * rows
    cap = slots // nt
    width = HEADS * HD
    row = lambda x: x.reshape(1, -1)
    patches = rows // PATCH
    inputs = (
        feats,
        row(occupancy),
        adjacency.transpose(0, 2, 1),
        row(serial_pos),
        conv_one,
        conv_two,
        row(gain_one),
        row(gain_two),
        row(gain_attn),
        w_qkv,
        w_out.T,
        row(gain_mlp),
        w_up.T,
        w_down,
    )
    return pl.pallas_call(
        functools.partial(kernel, nb, nt),
        out_shape=jax.ShapeDtypeStruct((channels, rows), BF16),
        in_specs=[pl.BlockSpec(memory_space=pltpu.HBM)] * INPUTS,
        out_specs=pl.BlockSpec(memory_space=pltpu.VMEM),
        scratch_shapes=[
            pltpu.SMEM(x.shape, x.dtype) if i == 2 else pltpu.VMEM(x.shape, x.dtype)
            for i, x in enumerate(inputs)
        ]
        + [
            pltpu.VMEM((channels, rows), BF16),
            pltpu.VMEM((7 * channels, rows), BF16),
            pltpu.VMEM((channels, 7 * channels), BF16),
            pltpu.VMEM((channels, rows), F32),
            pltpu.VMEM((rows, 512), BF16),
            pltpu.VMEM((rows, 768), BF16),
            pltpu.VMEM((2, 128, BLOCK), BF16),
            pltpu.VMEM((2, 4, channels, 128), BF16),
            pltpu.VMEM((2, 4, channels, 128), BF16),
            pltpu.VMEM((slots, rows), BF16),
            pltpu.VMEM((nt, 8, cap), F32),
            pltpu.VMEM((nt, 8, cap), F32),
            pltpu.VMEM((16, slots), BF16),
            pltpu.VMEM((rows, slots), BF16),
            pltpu.VMEM((channels, rows), BF16),
            pltpu.VMEM((nt, channels, cap), BF16),
            pltpu.VMEM((nt, channels, cap), BF16),
            pltpu.VMEM((channels + 16, rows), F32),
            pltpu.VMEM((rows, HEADS * 32), BF16),
            pltpu.VMEM((patches * HEADS, SET * 32, PATCH), BF16),
            pltpu.VMEM((HEADS * 16, rows), BF16),
            pltpu.VMEM((HEADS, 1, rows), F32),
            pltpu.VMEM((width, rows), F32),
            pltpu.VMEM((nt // GROUP, width, GROUP * cap), F32),
            pltpu.VMEM((nt, width, cap), BF16),
            pltpu.VMEM((nt, width, cap), BF16),
            pltpu.SemaphoreType.DMA((2, 2, 4)),
            pltpu.SemaphoreType.DMA((2, nt)),
            pltpu.SemaphoreType.DMA((2, nt)),
            pltpu.SemaphoreType.DMA((2, 2, nt)),
            pltpu.SemaphoreType.DMA((INPUTS,)),
        ],
        compiler_params=pltpu.CompilerParams(
            collective_id=0,
            has_side_effects=True,
            vmem_limit_bytes=VMEM_LIMIT,
        ),
        name="voxel_step",
    )(*[pltpu.with_memory_space_constraint(x, pltpu.HBM) for x in inputs])


def solution(mesh):
    nb, nt = mesh.shape["block"], mesh.shape["token"]
    split = ("block", "token")
    in_specs = (P(None, split), P(split), P(None, None, split), P(split)) + (P(),) * 10
    return jax.shard_map(
        functools.partial(per_device, nb, nt),
        mesh=mesh,
        in_specs=in_specs,
        out_specs=P(None, split),
        check_vma=False,
    )
```
